32 devices in a mesh: wide: 16 (over z, x, core), tensor: 2 (over y).
Axes of the slice: x: 2, y: 2, z: 4, core: 2. Of those that a mesh axis runs over, the one named last changes fastest.
Arguments:
- tokens: bfloat16 [50432, 384], P(('wide', 'tensor')), may hold values from -6 to 6
- ln1_gain: float32 [384], P('wide'), may hold values from 0.1 to 1.9
- qkv_weight: bfloat16 [384, 3, 384], P('wide', None, 'tensor'), may hold values from -0.3125 to 0.3125
- out_weight: bfloat16 [384, 384], P('tensor', 'wide'), may hold values from -0.875 to 0.875
- ln2_gain: float32 [384], P('wide'), may hold values from 0.1 to 1.9
- fc1_weight: bfloat16 [384, 1536], P('wide', 'tensor'), may hold values from -0.3125 to 0.3125
- fc2_weight: bfloat16 [1536, 384], P('tensor', 'wide'), may hold values from -0.15625 to 0.15625
- out_grad: bfloat16 [50432, 384], P(('wide', 'tensor')), may hold values from -6 to 6
Outputs:
- layer_out: bfloat16 [50432, 384], P(('wide', 'tensor'))
- input_token_gradient: float32 [50432, 384], P(('wide', 'tensor'))
- ln1_gain_grad: float32 [384], P('wide')
- qkv_weight_grad: float32 [384, 3, 384], P('wide', None, 'tensor')
- out_weight_grad: float32 [384, 384], P('tensor', 'wide')
- ln2_gain_grad: float32 [384], P('wide')
- fc1_weight_grad: float32 [384, 1536], P('wide', 'tensor')
- fc2_weight_grad: float32 [1536, 384], P('tensor', 'wide')
The draws below stay inside these ranges and needn't reach their ends.
All inputs are finite; a program needn't handle non-finite values.
Results may differ from the reference program's by a relative error of at most 0.035.
Values may be sent and summed in bfloat16 or wider, within the bound.
No kernel may reach another device: no remote copies, remote signals or barrier semaphores. Data moves between devices by JAX's collectives and lax.ppermute only.
A program may use at most 128 MiB of HBM per device.

```python
import jax
import jax.numpy as jnp
from jax import lax

H = 6
HD = 64
FF = 1536
SEQ = 197
D = 384
IMGS = 256
TOKENS = 50432


def block_scale(rng, shape, split, low, top_value):
    def one(axis_at, blocks):
        draws = jax.random.uniform(jax.random.fold_in(jax.random.fold_in(rng, 6), axis_at), (blocks,), jnp.float32, low / len(split), top_value / len(split))
        return jnp.repeat(jnp.exp(draws), shape[axis_at] // blocks).reshape((-1,) + (1,) * (len(shape) - axis_at - 1))

    factor_of = one(*split[0])
    for cut in split[1:]:
        factor_of = factor_of * one(*cut)
    return factor_of


def scatter_about(own_key, shape, scale, reach, pieces=(), dtype=jnp.bfloat16):
    entries = scale * jax.random.normal(own_key, shape, jnp.float32)
    if pieces:
        entries = entries * block_scale(own_key, shape, pieces, -0.22, 0.18)
    return jnp.clip(entries, -reach, reach).astype(dtype)


def setup_inputs(seed: int = 0) -> dict:
    key_of = jax.random.split(jax.random.key(seed), 9)
    tokens = scatter_about(key_of[0], (TOKENS, D), 1.0, 6.0, ((0, 32),))
    ln1_gain = jnp.clip(1.0 + 0.18 * jax.random.normal(key_of[1], (D,), jnp.float32), 0.1, 1.9)
    qkv_weight = scatter_about(key_of[2], (D, 3, D), D ** -0.5, 0.3125, ((0, 16), (2, 2)))
    out_weight = scatter_about(key_of[3], (D, D), (D // 8) ** -0.5, 0.875, ((0, 2), (1, 16)))
    ln2_gain = jnp.clip(1.0 + 0.18 * jax.random.normal(key_of[4], (D,), jnp.float32), 0.1, 1.9)
    fc1_weight = scatter_about(key_of[5], (D, FF), D ** -0.5, 0.3125, ((0, 16), (1, 2)))
    fc2_weight = scatter_about(key_of[6], (FF, D), FF ** -0.5, 0.15625, ((0, 2), (1, 16)))
    out_grad = scatter_about(key_of[7], (TOKENS, D), 1.0, 6.0, ((0, 32),))
    return {"tokens": tokens, "ln1_gain": ln1_gain, "qkv_weight": qkv_weight, "out_weight": out_weight, "ln2_gain": ln2_gain, "fc1_weight": fc1_weight, "fc2_weight": fc2_weight, "out_grad": out_grad}


@jax.custom_vjp
def low(v):
    return lax.optimization_barrier(v.astype(jnp.bfloat16)).astype(jnp.float32)

@jax.custom_vjp
def low_back(v):
    return v

def low_keep(v):
    return (low(v), None)

def low_pass(kept, grad):
    return (grad,)

def back_keep(v):
    return (v, None)

def back_low(kept, grad):
    return (low(grad),)
low.defvjp(low_keep, low_pass)
low_back.defvjp(back_keep, back_low)
HIGHEST_MODE = lax.Precision.HIGHEST

def apply_layer_norm(values):
    center = values - lax.optimization_barrier(jnp.mean(values, axis=-1, keepdims=True))
    spread = lax.optimization_barrier(jnp.mean(center * center, axis=-1, keepdims=True))
    return center * lax.rsqrt(spread + 1e-06)

def attend(blocks):
    queries, key_rows, value_rows = blocks
    scores = low_back(jnp.einsum('shd,thd->hst', queries, key_rows, precision=HIGHEST_MODE) * HD ** (-0.5))
    weights = jax.nn.softmax(scores, axis=-1)
    return jnp.einsum('hst,thd->shd', low(weights), value_rows, precision=HIGHEST_MODE)

def forward(input_tokens, ln1_gain, qkv_weight, out_weight, ln2_gain, fc1_weight, fc2_weight):
    first_normed_tokens = low(apply_layer_norm(input_tokens) * ln1_gain)
    projected = low_back(low(jnp.einsum('rd,dcf->rcf', first_normed_tokens, qkv_weight, precision=HIGHEST_MODE)))
    split_heads = projected.reshape(IMGS, SEQ, 3, H, HD)
    heads_out = lax.map(jax.checkpoint(attend), (split_heads[:, :, 0], split_heads[:, :, 1], split_heads[:, :, 2]))
    mixed = low_back(low(heads_out.reshape(TOKENS, D)))
    attn_branch = low_back(jnp.dot(mixed, out_weight, precision=HIGHEST_MODE))
    attention_residual = input_tokens + attn_branch
    second_normed_tokens = low(apply_layer_norm(attention_residual) * ln2_gain)
    hidden_pre = low_back(jnp.dot(second_normed_tokens, fc1_weight, precision=HIGHEST_MODE))
    hidden = low(jax.nn.gelu(hidden_pre, approximate=True))
    return attention_residual + low_back(jnp.dot(hidden, fc2_weight, precision=HIGHEST_MODE))

def reference(tokens, ln1_gain, qkv_weight, out_weight, ln2_gain, fc1_weight, fc2_weight, out_grad):
    primals = (tokens.astype(jnp.float32), ln1_gain.astype(jnp.float32), qkv_weight.astype(jnp.float32), out_weight.astype(jnp.float32), ln2_gain.astype(jnp.float32), fc1_weight.astype(jnp.float32), fc2_weight.astype(jnp.float32))
    result, pullback = jax.vjp(forward, *primals)
    grads = pullback(out_grad.astype(jnp.float32))
    return (result.astype(jnp.bfloat16), grads[0], grads[1], grads[2], grads[3], grads[4], grads[5], grads[6])
```

```python
import functools

import jax
import jax.numpy as jnp
from jax import lax
from jax.experimental import pallas as pl
from jax.experimental.pallas import tpu as pltpu
from jax.sharding import PartitionSpec as P

HD = 64
SEQ = 197
PAD = 208
D = 384
QC = 640
F32 = jnp.float32
BF16 = jnp.bfloat16
NT = (((1,), (1,)), ((), ()))
TN = (((0,), (0,)), ((), ()))
GELU_C = 0.7978845608028654
VMEM_LIMIT = 60 * 1024 * 1024


def dot(a, b, dims=(((1,), (0,)), ((), ()))):
    return lax.dot_general(a, b, dims, preferred_element_type=F32)


def stage_bits(wide):
    bits = [("wide", 1 << k) for k in range(1, wide.bit_length() - 1)]
    bits = bits[1:] + bits[:1]
    return bits + [("tensor", 1), ("wide", 1)]


def relative(stages):
    places = [(0, 0)]
    for axis, bit in stages:
        places = places + [(w ^ bit, t) if axis == "wide" else (w, t ^ bit) for w, t in places]
    return places


def swap(value, stage, sizes):
    axis, bit = stage
    return lax.ppermute(value, axis, [(i, i ^ bit) for i in range(sizes[axis])])


def gather(block, stages, sizes):
    held = block[None]
    for stage in stages:
        held = jnp.concatenate([held, swap(held, stage, sizes)], axis=0)
    return held


def scatter_sum(blocks, stages, sizes):
    held = blocks
    for stage in reversed(stages):
        half = held.shape[0] // 2
        got = swap(held[half:], stage, sizes)
        total = held[:half].astype(F32) + got.astype(F32)
        held = total if half == 1 else total.astype(BF16)
    return held[0]


def in_order(places, held):
    me_w, me_t = lax.axis_index("wide"), lax.axis_index("tensor")
    at = {place: p for p, place in enumerate(places)}
    wide = len(places) // 2
    table = jnp.array([[at[w, t] for w in range(wide)] for t in range(2)], jnp.int32)
    order = table[me_t ^ jnp.arange(2)[:, None], me_w ^ jnp.arange(wide)[None, :]]
    return held[order.reshape(-1)].reshape(16, 48, held.shape[2])


def out_of_order(places, blocks, rows):
    me_w, me_t = lax.axis_index("wide"), lax.axis_index("tensor")
    wide = len(places) // 2
    order = jnp.array([w for w, _ in places], jnp.int32) ^ me_w
    order += wide * (jnp.array([t for _, t in places], jnp.int32) ^ me_t)
    return blocks.reshape(len(places), rows, blocks.shape[2])[order]


def rows_of(places, rows):
    if rows == 48:
        me_w, me_t = 0, 0
        places = [(w, t) for t in range(2) for w in range(8)]
    else:
        me_w, me_t = lax.axis_index("wide"), lax.axis_index("tensor")
    for p, (w, t) in enumerate(places):
        start = (me_w ^ w) * rows
        if rows % 8 == 0:
            start = pl.multiple_of(start, 8)
        yield p, me_t ^ t, pl.ds(start, rows)


def normalize(v):
    center = v - jnp.mean(v, axis=-1, keepdims=True)
    rstd = lax.rsqrt(jnp.mean(center * center, axis=-1, keepdims=True) + 1e-06)
    return center * rstd, rstd


def norm_back(grad, xhat, rstd, gain):
    g = grad * gain
    return rstd * (
        g
        - jnp.mean(g, axis=-1, keepdims=True)
        - xhat * jnp.mean(g * xhat, axis=-1, keepdims=True)
    )


def head_masks(shape):
    lane = lax.broadcasted_iota(jnp.int32, shape, len(shape) - 1)
    return lane < HD


def pick(value, low, side):
    zero = jnp.zeros_like(value)
    return jnp.where(low, value, zero) if side == 0 else jnp.where(low, zero, value)


def attend_kernel(places, rows, buf, x_ref, qkv_ref, probs_ref, heads_ref, n1_ref, w_ref, gain_ref, scr):
    @pl.when(pl.program_id(0) == 0)
    def _():
        for p, t, where in rows_of(places, rows):
            scr[t, where, :] = buf[p].astype(F32)
        for c in range(3):
            at = c * D
            w_ref[:, at : at + 128] = scr[0, :, c * 128 : c * 128 + 128].astype(BF16)
            w_ref[:, at + 128 : at + 256] = scr[1, :, c * 128 : c * 128 + 128].astype(BF16)
            one = 384 + c * HD
            last = jnp.concatenate([scr[0, :, one : one + HD], scr[1, :, one : one + HD]], axis=1)
            w_ref[:, at + 256 : at + 384] = last.astype(BF16)
        turned = scr[0, :, 512:640].T
        gain_ref[...] = turned[HD : HD + 8, :]

    xhat, _ = normalize(x_ref[0].astype(F32))
    n1 = (xhat * gain_ref[0:1, :]).astype(BF16)
    n1_ref[0] = n1
    proj = dot(n1, w_ref[...])
    low = head_masks((PAD, 128))
    key_ok = lax.broadcasted_iota(jnp.int32, (PAD, PAD), 0) < SEQ
    for c in range(3):
        at = slice(c * 128, c * 128 + 128)
        q = (proj[:, at] * (HD**-0.5)).astype(BF16)
        k = proj[:, D + c * 128 : D + c * 128 + 128].astype(BF16)
        v = proj[:, 2 * D + c * 128 : 2 * D + c * 128 + 128].astype(BF16)
        qkv_ref[0, :, at] = q
        qkv_ref[0, :, D + c * 128 : D + c * 128 + 128] = k
        qkv_ref[0, :, 2 * D + c * 128 : 2 * D + c * 128 + 128] = v
        v_turned = v.T
        parts = []
        for side in range(2):
            scores = dot(pick(k, low, side), q, NT)
            scores = jnp.where(key_ok, scores, -1e30)
            expon = jnp.exp(scores - jnp.max(scores, axis=0, keepdims=True))
            probs = expon * (1.0 / jnp.sum(expon, axis=0, keepdims=True))
            probs = probs.astype(BF16)
            probs_ref[0, 2 * c + side] = probs
            parts.append(dot(v_turned[side * HD : side * HD + HD, :], probs))
        heads_ref[0, :, at] = jnp.concatenate(parts, axis=0).T.astype(BF16)


def mlp_kernel(
    places, rows, images, fs, buf, x_ref, og_ref, h_ref, gain_ref,
    mid_ref, hid_ref, mg_ref, hg_ref, fc2_ref, out_ref,
    scr, w_out, w_fc1, n2_all, pg_all, hid_all, og_all, ml_all, h_all,
):
    step = pl.program_id(0)
    half = fs

    @pl.when(step == 0)
    def _():
        for p, t, where in rows_of(places, rows):
            scr[t, where, :] = buf[p].astype(F32)
        w_out[:, 0:128] = scr[0, :, 0:128].astype(BF16)
        w_out[:, 128:256] = scr[1, :, 0:128].astype(BF16)
        w_out[:, 256:384] = jnp.concatenate([scr[0, :, 128:192], scr[1, :, 128:192]], axis=1).astype(BF16)
        for t in range(2):
            w_fc1[:, t * half : t * half + half] = scr[t, :, 256 : 256 + half].astype(BF16)
            fc2_ref[:, t * half : t * half + half] = scr[t, :, 256 + half :].astype(BF16)

    @pl.when(step < images)
    def _():
        at = pl.ds(pl.multiple_of(step * PAD, PAD), PAD)
        gain = gain_ref[1:2, :]
        h = h_ref[0]
        og = og_ref[0]
        h_all[at, :] = h
        og_all[at, :] = og
        middle = x_ref[0].astype(F32) + dot(h, w_out[...], NT)
        mid_ref[0] = middle
        xhat, rstd = normalize(middle)
        n2 = (xhat * gain).astype(BF16)
        n2_all[at, :] = n2
        width = w_fc1.shape[1] // 2
        back = None
        for c in range(2):
            cols = slice(c * width, c * width + width)
            u = dot(n2, w_fc1[:, cols])
            square = u * u
            bent = jnp.tanh(GELU_C * u * (1.0 + 0.044715 * square))
            hid = (0.5 * u * (1.0 + bent)).astype(BF16)
            hid_ref[0, :, cols] = hid
            hid_all[at, cols] = hid
            slope = 0.5 * (1.0 + bent) + 0.5 * u * (1.0 - bent * bent) * (GELU_C * (1.0 + 0.134145 * square))
            pg = (dot(og, fc2_ref[:, cols]) * slope).astype(BF16)
            pg_all[at, cols] = pg
            part = dot(pg, w_fc1[:, cols], NT)
            back = part if back is None else back + part
        mg = og.astype(F32) + norm_back(back, xhat, rstd, gain)
        mg_ref[0] = mg
        ml = mg.astype(BF16)
        ml_all[at, :] = ml
        hg_ref[0] = dot(ml, w_out[...]).astype(BF16)

    @pl.when(step == images)
    def _():
        turned = n2_all[...].T
        row_sum = jnp.zeros((D, 1), F32)
        chunk = half // 3
        for t in range(2):
            for c in range(3):
                cols = slice(t * half + c * chunk, t * half + c * chunk + chunk)
                grad = dot(turned, pg_all[:, cols])
                scr[t, :, 256 + c * chunk : 256 + c * chunk + chunk] = grad
                row_sum += jnp.sum(grad * w_fc1[:, cols].astype(F32), axis=1, keepdims=True)
        turned = og_all[...].T
        for t in range(2):
            for c in range(3):
                cols = slice(t * half + c * chunk, t * half + c * chunk + chunk)
                scr[t, :, 256 + half + c * chunk : 256 + half + c * chunk + chunk] = dot(turned, hid_all[:, cols])
        grad = dot(ml_all[...].T, h_all[...])
        scr[0, :, 0:128] = grad[:, 0:128]
        scr[1, :, 0:128] = grad[:, 128:256]
        gain = jnp.broadcast_to(row_sum, (D, HD))
        scr[0, :, 128:256] = jnp.concatenate([grad[:, 256 : 256 + HD], gain], axis=1)
        scr[1, :, 128:256] = jnp.concatenate([grad[:, 256 + HD : 384], gain], axis=1)
        for p, t, where in rows_of(places, rows):
            out_ref[p] = scr[t, where, :].astype(BF16)


def attend_back_kernel(
    places, rows, images, qkv_ref, probs_ref, hg_ref, n1_ref, w_ref, grad_ref, out_ref, scr, n1_all, grad_all
):
    step = pl.program_id(0)

    @pl.when(step < images)
    def _():
        at = pl.ds(pl.multiple_of(step * PAD, PAD), PAD)
        n1_all[at, :] = n1_ref[0]
        low = head_masks((PAD, 128))
        for c in range(3):
            cols = slice(c * 128, c * 128 + 128)
            kcols = slice(D + c * 128, D + c * 128 + 128)
            vcols = slice(2 * D + c * 128, 2 * D + c * 128 + 128)
            q, k, v = qkv_ref[0, :, cols], qkv_ref[0, :, kcols], qkv_ref[0, :, vcols]
            do = hg_ref[0, :, cols]
            k_turned = k.T
            dq, dk, dv = [], [], []
            for side in range(2):
                probs_low = probs_ref[0, 2 * c + side]
                probs = probs_low.astype(F32)
                dp = dot(pick(v, low, side), do, NT)
                ds = probs * (dp - jnp.sum(probs * dp, axis=0, keepdims=True))
                ds = ds.astype(BF16)
                dv.append(dot(probs_low, do))
                dk.append(dot(ds, q))
                dq.append(dot(k_turned[side * HD : side * HD + HD, :], ds))
            for span, value in (
                (cols, jnp.concatenate(dq, axis=0).T * (HD**-0.5)),
                (kcols, jnp.where(low, dk[0], dk[1])),
                (vcols, jnp.where(low, dv[0], dv[1])),
            ):
                value = value.astype(BF16)
                grad_ref[0, :, span] = value
                grad_all[at, span] = value

    @pl.when(step == images)
    def _():
        turned = n1_all[...].T
        row_sum = jnp.zeros((D, 1), F32)
        singles = []
        for c in range(3):
            span = slice(c * D, c * D + D)
            grad = dot(turned, grad_all[:, span])
            row_sum += jnp.sum(grad * w_ref[:, span].astype(F32), axis=1, keepdims=True)
            scr[0, :, c * 128 : c * 128 + 128] = grad[:, 0:128]
            scr[1, :, c * 128 : c * 128 + 128] = grad[:, 128:256]
            singles.append(grad[:, 256:384])
        gain = jnp.broadcast_to(row_sum, (D, HD))
        for t in range(2):
            own = [s[:, t * HD : t * HD + HD] for s in singles]
            scr[t, :, 384:512] = jnp.concatenate(own[:2], axis=1)
            scr[t, :, 512:640] = jnp.concatenate([own[2], gain], axis=1)
        for p, t, where in rows_of(places, rows):
            out_ref[p] = scr[t, where, :].astype(BF16)


def input_grad_kernel(grad_ref, w_ref, x_ref, mg_ref, gain_ref, out_ref):
    xhat, rstd = normalize(x_ref[0].astype(F32))
    back = dot(grad_ref[0], w_ref[...], NT)
    out_ref[0] = mg_ref[0] + norm_back(back, xhat, rstd, gain_ref[0:1, :])


def layer_out_kernel(hid_ref, fc2_ref, mid_ref, out_ref):
    out_ref[0] = (mid_ref[0] + dot(hid_ref[0], fc2_ref[...], NT)).astype(BF16)


def whole(*shape):
    return pl.BlockSpec(shape, lambda i: (0,) * len(shape))


def per_image(images, *shape):
    return pl.BlockSpec((1,) + shape, lambda i: (jnp.minimum(i, images - 1),) + (0,) * len(shape))


def call(kernel, grid, ins, outs, scratch, args, name, flops, nbytes):
    return pl.pallas_call(
        kernel,
        grid=(grid,),
        in_specs=ins,
        out_specs=[spec for spec, _ in outs],
        out_shape=[shape for _, shape in outs],
        scratch_shapes=scratch,
        compiler_params=pltpu.CompilerParams(vmem_limit_bytes=VMEM_LIMIT),
        cost_estimate=pl.CostEstimate(flops=flops, bytes_accessed=nbytes, transcendentals=0),
        name=name,
    )(*args)


def shape_of(*shape, dtype=BF16):
    return jax.ShapeDtypeStruct(shape, dtype)


def local(sizes, tokens, ln1_gain, qkv_weight, out_weight, ln2_gain, fc1_weight, fc2_weight, out_grad):
    stages = stage_bits(sizes["wide"])
    places = relative(stages)
    n = len(places)
    rows = qkv_weight.shape[0]
    images = tokens.shape[0] // SEQ
    fs = fc1_weight.shape[1]
    ff = 2 * fs
    rc = 256 + 2 * fs

    gains = jnp.stack([ln1_gain, ln2_gain], axis=1).astype(BF16)
    first = jnp.concatenate(
        [qkv_weight[:, c, 0:128] for c in range(3)]
        + [qkv_weight[:, c, 128:192] for c in range(3)]
        + [gains, jnp.zeros((rows, HD - 2), BF16)],
        axis=1,
    )
    rest = jnp.concatenate(
        [out_weight.T, jnp.zeros((rows, HD), BF16), fc1_weight, fc2_weight.T], axis=1
    )
    first_all = gather(first, stages, sizes)
    rest_all = gather(rest, stages, sizes)
    own_rows = rows
    if rows % 8 != 0:
        first_all, rest_all = in_order(places, first_all), in_order(places, rest_all)
        n, rows = 16, 48

    pads = ((0, 0), (0, PAD - SEQ), (0, 0))
    x = jnp.pad(tokens.reshape(images, SEQ, D), pads)
    og = jnp.pad(out_grad.reshape(images, SEQ, D), pads)

    row = functools.partial(per_image, images)
    big = images * PAD
    qkv, probs, heads, n1, w_qkv, gain = call(
        functools.partial(attend_kernel, places, rows),
        images,
        [whole(n, rows, QC), row(PAD, D)],
        [
            (row(PAD, 3 * D), shape_of(images, PAD, 3 * D)),
            (row(6, PAD, PAD), shape_of(images, 6, PAD, PAD)),
            (row(PAD, D), shape_of(images, PAD, D)),
            (row(PAD, D), shape_of(images, PAD, D)),
            (whole(D, 3 * D), shape_of(D, 3 * D)),
            (whole(8, D), shape_of(8, D, dtype=F32)),
        ],
        [pltpu.VMEM((2, D, QC), F32)],
        (first_all, x),
        "attend",
        8 * 10**9,
        20 * 10**6,
    )
    middle, hid, mg, hg, fc2_t, rest_grad = call(
        functools.partial(mlp_kernel, places, rows, images, fs),
        images + 1,
        [whole(n, rows, rc), row(PAD, D), row(PAD, D), row(PAD, D), whole(8, D)],
        [
            (row(PAD, D), shape_of(images, PAD, D, dtype=F32)),
            (row(PAD, ff), shape_of(images, PAD, ff)),
            (row(PAD, D), shape_of(images, PAD, D, dtype=F32)),
            (row(PAD, D), shape_of(images, PAD, D)),
            (whole(D, ff), shape_of(D, ff)),
            (whole(n, rows, rc), shape_of(n, rows, rc)),
        ],
        [
            pltpu.VMEM((2, D, rc), F32),
            pltpu.VMEM((D, D), BF16),
            pltpu.VMEM((D, ff), BF16),
            pltpu.VMEM((big, D), BF16),
            pltpu.VMEM((big, ff), BF16),
            pltpu.VMEM((big, ff), BF16),
            pltpu.VMEM((big, D), BF16),
            pltpu.VMEM((big, D), BF16),
            pltpu.VMEM((big, D), BF16),
        ],
        (rest_all, x, og, heads, gain),
        "mlp",
        14 * 10**9,
        30 * 10**6,
    )
    grads, first_grad = call(
        functools.partial(attend_back_kernel, places, rows, images),
        images + 1,
        [row(PAD, 3 * D), row(6, PAD, PAD), row(PAD, D), row(PAD, D), whole(D, 3 * D)],
        [
            (row(PAD, 3 * D), shape_of(images, PAD, 3 * D)),
            (whole(n, rows, QC), shape_of(n, rows, QC)),
        ],
        [
            pltpu.VMEM((2, D, QC), F32),
            pltpu.VMEM((big, D), BF16),
            pltpu.VMEM((big, 3 * D), BF16),
        ],
        (qkv, probs, hg, n1, w_qkv),
        "attend_back",
        8 * 10**9,
        20 * 10**6,
    )
    (dx,) = call(
        input_grad_kernel,
        images,
        [row(PAD, 3 * D), whole(D, 3 * D), row(PAD, D), row(PAD, D), whole(8, D)],
        [(row(PAD, D), shape_of(images, PAD, D, dtype=F32))],
        [],
        (grads, w_qkv, x, mg, gain),
        "input_grad",
        2 * 10**9,
        10 * 10**6,
    )
    (y,) = call(
        layer_out_kernel,
        images,
        [row(PAD, ff), whole(D, ff), row(PAD, D)],
        [(row(PAD, D), shape_of(images, PAD, D))],
        [],
        (hid, fc2_t, middle),
        "layer_out",
        2 * 10**9,
        10 * 10**6,
    )

    if rows != own_rows:
        rest_grad = out_of_order(places, rest_grad, own_rows)
        first_grad = out_of_order(places, first_grad, own_rows)
    rest_sum = scatter_sum(rest_grad, stages, sizes)
    first_sum = scatter_sum(first_grad, stages, sizes)
    kept1 = ln1_gain.astype(BF16).astype(F32)
    kept2 = ln2_gain.astype(BF16).astype(F32)
    qkv_shard = jnp.stack(
        [
            jnp.concatenate(
                [first_sum[:, c * 128 : c * 128 + 128], first_sum[:, 384 + c * HD : 448 + c * HD]],
                axis=1,
            )
            for c in range(3)
        ],
        axis=1,
    )
    return (
        y[:, :SEQ].reshape(-1, D),
        dx[:, :SEQ].reshape(-1, D),
        first_sum[:, 576] / kept1,
        qkv_shard,
        rest_sum[:, :192].T,
        rest_sum[:, 192] / kept2,
        rest_sum[:, 256 : 256 + fs],
        rest_sum[:, 256 + fs :].T,
    )


def solution(mesh):
    rows = P(("wide", "tensor"), None)
    weights = (
        P("wide"),
        P("wide", None, "tensor"),
        P("tensor", "wide"),
        P("wide"),
        P("wide", "tensor"),
        P("tensor", "wide"),
    )
    return jax.shard_map(
        functools.partial(local, dict(mesh.shape)),
        mesh=mesh,
        in_specs=(rows, *weights, rows),
        out_specs=(rows, rows, *weights),
        check_vma=False,
    )
```

```python
import functools

import jax
import jax.numpy as jnp
from jax import lax
from jax.experimental import pallas as pl
from jax.experimental.pallas import tpu as pltpu
from jax.sharding import PartitionSpec as P

HD = 64
SEQ = 197
PAD = 208
PER = 2
D = 384
QC = 640
F32 = jnp.float32
BF16 = jnp.bfloat16
NT = (((1,), (1,)), ((), ()))
GELU_C = 0.7978845608028654
VMEM_LIMIT = 60 * 1024 * 1024


def dot(a, b, dims=(((1,), (0,)), ((), ()))):
    return lax.dot_general(a, b, dims, preferred_element_type=F32)


def stage_bits(wide):
    bits = [("wide", 1 << k) for k in range(1, wide.bit_length() - 1)]
    bits = bits[:0:-1] + bits[:1]
    return bits + [("tensor", 1), ("wide", 1)]


def relative(stages):
    places = [(0, 0)]
    for axis, bit in stages:
        places = places + [(w ^ bit, t) if axis == "wide" else (w, t ^ bit) for w, t in places]
    return places


def swap(value, stage, sizes):
    axis, bit = stage
    return lax.ppermute(value, axis, [(i, i ^ bit) for i in range(sizes[axis])])


def gather(block, stages, sizes):
    held = block
    for stage in stages[:-2]:
        got = swap(held, stage, sizes)
        held = jnp.concatenate([held, got], axis=0)
    got = swap(held, stages[-2], sizes)
    return [held, got, swap(held, stages[-1], sizes), swap(got, stages[-1], sizes)]


def half_sum(keep, send, stage, sizes):
    got = swap(send, stage, sizes)
    total = (keep.astype(F32) + got.astype(F32)).astype(BF16)
    half = total.shape[0] // 2
    return total[:half], total[half:]


def in_order(places, held):
    me_w, me_t = lax.axis_index("wide"), lax.axis_index("tensor")
    at = {place: p for p, place in enumerate(places)}
    wide = len(places) // 2
    table = jnp.array([[at[w, t] for w in range(wide)] for t in range(2)], jnp.int32)
    order = table[me_t ^ jnp.arange(2)[:, None], me_w ^ jnp.arange(wide)[None, :]]
    return held[order.reshape(-1)].reshape(16, 48, held.shape[2])


def out_of_order(places, blocks, rows):
    me_w, me_t = lax.axis_index("wide"), lax.axis_index("tensor")
    wide = len(places) // 2
    order = jnp.array([w for w, _ in places], jnp.int32) ^ me_w
    order += wide * (jnp.array([t for _, t in places], jnp.int32) ^ me_t)
    return blocks.reshape(len(places), rows, blocks.shape[2])[order]


def rows_of(places, rows):
    if rows == 48:
        me_w, me_t = 0, 0
        places = [(w, t) for t in range(2) for w in range(8)]
    else:
        me_w, me_t = lax.axis_index("wide"), lax.axis_index("tensor")
    for p, (w, t) in enumerate(places):
        yield p, me_t ^ t, pl.ds(pl.multiple_of((me_w ^ w) * rows, 8), rows)


def unpack(places, rows, pieces, scr, at=0):
    size = len(pieces[0])
    width = pieces[0].shape[-1]
    for p, t, where in rows_of(places, rows):
        scr[t, where, at : at + width] = pieces[p // size][p % size].astype(F32)


def repack(places, rows, scr, pieces, at=0):
    size = len(pieces[0])
    width = pieces[0].shape[-1]
    for p, t, where in rows_of(places, rows):
        pieces[p // size][p % size] = scr[t, where, at : at + width].astype(BF16)


def normalize(v):
    center = v - jnp.mean(v, axis=-1, keepdims=True)
    rstd = lax.rsqrt(jnp.mean(center * center, axis=-1, keepdims=True) + 1e-06)
    return center * rstd, rstd


def norm_back(grad, xhat, rstd, gain):
    g = grad * gain
    return rstd * (
        g
        - jnp.mean(g, axis=-1, keepdims=True)
        - xhat * jnp.mean(g * xhat, axis=-1, keepdims=True)
    )


def low_lanes():
    return lax.broadcasted_iota(jnp.int32, (PAD, 128), 1) < HD


def pick(value, low, side):
    zero = jnp.zeros_like(value)
    return jnp.where(low, value, zero) if side == 0 else jnp.where(low, zero, value)


def tall(ref):
    return ref[...].reshape(PER * PAD, ref.shape[-1])


def column(row):
    n = row.shape[1]
    own = lax.broadcasted_iota(jnp.int32, (n, n), 0) == lax.broadcasted_iota(jnp.int32, (n, n), 1)
    return jnp.sum(jnp.where(own, jnp.broadcast_to(row, (n, n)), 0.0), axis=1, keepdims=True)


def line(col):
    n = col.shape[0]
    own = lax.broadcasted_iota(jnp.int32, (n, n), 0) == lax.broadcasted_iota(jnp.int32, (n, n), 1)
    return jnp.sum(jnp.where(own, jnp.broadcast_to(col, (n, n)), 0.0), axis=0, keepdims=True)


def pack_kernel(qkv, gain1, gain2, out, fc1, fc2, first, rest):
    rows = out.shape[0]
    fs = fc1.shape[1]
    lane = lax.broadcasted_iota(jnp.int32, (rows, HD), 1)
    gains = jnp.where(lane == 0, column(gain1[...]), jnp.where(lane == 1, column(gain2[...]), 0.0))
    for c in range(3):
        first[0, :, c * 128 : c * 128 + 128] = qkv[c, :, 0:128]
    single = [qkv[c, :, 128:192].astype(F32) for c in range(3)]
    first[0, :, 384:512] = jnp.concatenate(single[:2], axis=1).astype(BF16)
    first[0, :, 512:640] = jnp.concatenate([single[2], gains], axis=1).astype(BF16)
    rest[0, :, 0:128] = out[:, 0:128]
    pad = jnp.zeros((rows, HD), F32)
    rest[0, :, 128:256] = jnp.concatenate([out[:, 128:192].astype(F32), pad], axis=1).astype(BF16)
    rest[0, :, 256 : 256 + fs] = fc1[...]
    rest[0, :, 256 + fs :] = fc2[...]


def attend_kernel(places, rows, p0, p1, p2, p3, x_ref, qkv_ref, probs_ref, heads_ref, n1_ref, w_ref, gain_ref, scr):
    @pl.when(pl.program_id(0) == 0)
    def _():
        unpack(places, rows, (p0, p1, p2, p3), scr)
        for c in range(3):
            at = c * D
            w_ref[:, at : at + 128] = scr[0, :, c * 128 : c * 128 + 128].astype(BF16)
            w_ref[:, at + 128 : at + 256] = scr[1, :, c * 128 : c * 128 + 128].astype(BF16)
            one = 384 + c * HD
            last = jnp.concatenate([scr[0, :, one : one + HD], scr[1, :, one : one + HD]], axis=1)
            w_ref[:, at + 256 : at + 384] = last.astype(BF16)
        turned = scr[0, :, 512:640].T
        gain_ref[...] = turned[HD : HD + 8, :]

    xhat, _ = normalize(tall(x_ref).astype(F32))
    n1 = (xhat * gain_ref[0:1, :]).astype(BF16)
    n1_ref[...] = n1.reshape(PER, PAD, D)
    proj = dot(n1, w_ref[...])
    low = low_lanes()
    key_ok = lax.broadcasted_iota(jnp.int32, (PAD, PAD), 0) < SEQ
    for i in range(PER):
        mine = slice(i * PAD, i * PAD + PAD)
        for c in range(3):
            at = slice(c * 128, c * 128 + 128)
            q = (proj[mine, at] * (HD**-0.5)).astype(BF16)
            k = proj[mine, D + c * 128 : D + c * 128 + 128].astype(BF16)
            v = proj[mine, 2 * D + c * 128 : 2 * D + c * 128 + 128].astype(BF16)
            qkv_ref[i, :, at] = q
            qkv_ref[i, :, D + c * 128 : D + c * 128 + 128] = k
            qkv_ref[i, :, 2 * D + c * 128 : 2 * D + c * 128 + 128] = v
            v_turned = v.T
            parts = []
            for side in range(2):
                scores = dot(pick(k, low, side), q, NT)
                scores = jnp.where(key_ok, scores, -1e30)
                expon = jnp.exp(scores - jnp.max(scores, axis=0, keepdims=True))
                probs = expon * (1.0 / jnp.sum(expon, axis=0, keepdims=True))
                probs = probs.astype(BF16)
                probs_ref[i, 2 * c + side] = probs
                parts.append(dot(v_turned[side * HD : side * HD + HD, :], probs))
            heads_ref[i, :, at] = jnp.concatenate(parts, axis=0).T.astype(BF16)


def mlp_kernel(
    places, places2, rows, blocks, fs, p0, p1, p2, p3, x_ref, og_ref, h_ref, gain_ref,
    mid_ref, hid_ref, mg_ref, hg_ref, fc2_ref, keep1, send1, keep2, send2,
    scr, w_out, w_back, w_fc1, w_fc1_turned, n2_all, pg_all, hid_all, og_all, ml_all, h_all,
):
    step = pl.program_id(0)

    @pl.when(step == 0)
    def _():
        unpack(places, rows, (p0, p1, p2, p3), scr)
        last = jnp.concatenate([scr[0, :, 128:192], scr[1, :, 128:192]], axis=1)
        for b, value in enumerate((scr[0, :, 0:128], scr[1, :, 0:128], last)):
            w_back[:, b * 128 : b * 128 + 128] = value.astype(BF16)
            w_out[b * 128 : b * 128 + 128, :] = value.T.astype(BF16)
        for t in range(2):
            at = slice(t * fs, t * fs + fs)
            w_fc1[:, at] = scr[t, :, 256 : 256 + fs].astype(BF16)
            w_fc1_turned[at, :] = scr[t, :, 256 : 256 + fs].T.astype(BF16)
            fc2_ref[:, at] = scr[t, :, 256 + fs :].astype(BF16)

    @pl.when(step < blocks)
    def _():
        size = PER * PAD
        at = pl.ds(pl.multiple_of(step * size, size), size)
        gain = gain_ref[1:2, :]
        h = tall(h_ref)
        og = tall(og_ref)
        h_all[at, :] = h
        og_all[at, :] = og
        middle = tall(x_ref).astype(F32) + dot(h, w_out[...])
        mid_ref[...] = middle.reshape(PER, PAD, D)
        xhat, rstd = normalize(middle)
        n2 = (xhat * gain).astype(BF16)
        n2_all[at, :] = n2
        width = fs // 2
        back = None
        for c in range(4):
            cols = slice(c * width, c * width + width)
            u = dot(n2, w_fc1[:, cols])
            square = u * u
            bent = jnp.tanh(u * (GELU_C + (GELU_C * 0.044715) * square))
            plus = 0.5 + 0.5 * bent
            hid = (u * plus).astype(BF16)
            hid_ref[:, :, cols] = hid.reshape(PER, PAD, width)
            hid_all[at, cols] = hid
            slope = plus * (1.0 + u * (1.0 - bent) * (GELU_C + (GELU_C * 0.134145) * square))
            pg = (dot(og, fc2_ref[:, cols]) * slope).astype(BF16)
            pg_all[at, cols] = pg
            part = dot(pg, w_fc1_turned[cols, :])
            back = part if back is None else back + part
        mg = og.astype(F32) + norm_back(back, xhat, rstd, gain)
        mg_ref[...] = mg.reshape(PER, PAD, D)
        ml = mg.astype(BF16)
        ml_all[at, :] = ml
        hg_ref[...] = dot(ml, w_back[...]).astype(BF16).reshape(PER, PAD, D)

    @pl.when(step == blocks)
    def _():
        turned = n2_all[...].T
        row_sum = jnp.zeros((D, 1), F32)
        chunk = fs // 3
        for t in range(2):
            for c in range(3):
                cols = slice(t * fs + c * chunk, t * fs + c * chunk + chunk)
                grad = dot(turned, pg_all[:, cols])
                scr[t, :, 256 + c * chunk : 256 + c * chunk + chunk] = grad
                row_sum += jnp.sum(grad * w_fc1[:, cols].astype(F32), axis=1, keepdims=True)
        turned = og_all[...].T
        for t in range(2):
            for c in range(3):
                cols = slice(t * fs + c * chunk, t * fs + c * chunk + chunk)
                scr[t, :, 256 + fs + c * chunk : 256 + fs + c * chunk + chunk] = dot(turned, hid_all[:, cols])
        grad = dot(ml_all[...].T, h_all[...])
        scr[0, :, 0:128] = grad[:, 0:128]
        scr[1, :, 0:128] = grad[:, 128:256]
        gain = jnp.broadcast_to(row_sum, (D, HD))
        scr[0, :, 128:256] = jnp.concatenate([grad[:, 256 : 256 + HD], gain], axis=1)
        scr[1, :, 128:256] = jnp.concatenate([grad[:, 256 + HD : 384], gain], axis=1)
        repack(places, rows, scr, (keep1, send1))
        repack(places2, rows, scr, (keep2, send2), 256 + fs)


def attend_back(qkv_ref, probs_ref, hg_ref, grad_ref, grad_all, at):
    low = low_lanes()
    for i in range(PER):
        for c in range(3):
            cols = slice(c * 128, c * 128 + 128)
            kcols = slice(D + c * 128, D + c * 128 + 128)
            vcols = slice(2 * D + c * 128, 2 * D + c * 128 + 128)
            q, k, v = qkv_ref[i, :, cols], qkv_ref[i, :, kcols], qkv_ref[i, :, vcols]
            do = hg_ref[i, :, cols]
            k_turned = k.T
            dq, dk, dv = [], [], []
            for side in range(2):
                probs_low = probs_ref[i, 2 * c + side]
                probs = probs_low.astype(F32)
                dp = dot(pick(v, low, side), do, NT)
                ds = probs * (dp - jnp.sum(probs * dp, axis=0, keepdims=True))
                ds = ds.astype(BF16)
                dv.append(dot(probs_low, do))
                dk.append(dot(ds, q))
                dq.append(dot(k_turned[side * HD : side * HD + HD, :], ds))
            for span, value in (
                (cols, jnp.concatenate(dq, axis=0).T * (HD**-0.5)),
                (kcols, jnp.where(low, dk[0], dk[1])),
                (vcols, jnp.where(low, dv[0], dv[1])),
            ):
                value = value.astype(BF16)
                grad_ref[i, :, span] = value
                if grad_all is not None:
                    grad_all[pl.ds(pl.multiple_of(at + i * PAD, PAD), PAD), span] = value


def attend_back_kernel(qkv_ref, probs_ref, hg_ref, grad_ref):
    attend_back(qkv_ref, probs_ref, hg_ref, grad_ref, None, 0)


def attend_last_kernel(
    places, rows, blocks, qkv_ref, probs_ref, hg_ref, n1_ref, w_ref, *refs
):
    *earlier, grad_ref, keep, send, scr, grad_all = refs
    step = pl.program_id(0)
    early = sum(ref.shape[0] for ref in earlier) * PAD

    @pl.when(step == 0)
    def _():
        at = 0
        for ref in earlier:
            size = ref.shape[0] * PAD
            grad_all[at : at + size, :] = ref[...].reshape(size, 3 * D)
            at += size

    @pl.when(step < blocks)
    def _():
        attend_back(qkv_ref, probs_ref, hg_ref, grad_ref, grad_all, early + step * PER * PAD)

    @pl.when(step == blocks)
    def _():
        turned = n1_ref[...].reshape(-1, D).T
        row_sum = jnp.zeros((D, 1), F32)
        singles = []
        for c in range(3):
            span = slice(c * D, c * D + D)
            grad = dot(turned, grad_all[:, span])
            row_sum += jnp.sum(grad * w_ref[:, span].astype(F32), axis=1, keepdims=True)
            scr[0, :, c * 128 : c * 128 + 128] = grad[:, 0:128]
            scr[1, :, c * 128 : c * 128 + 128] = grad[:, 128:256]
            singles.append(grad[:, 256:384])
        gain = jnp.broadcast_to(row_sum, (D, HD))
        for t in range(2):
            own = [s[:, t * HD : t * HD + HD] for s in singles]
            scr[t, :, 384:512] = jnp.concatenate(own[:2], axis=1)
            scr[t, :, 512:640] = jnp.concatenate([own[2], gain], axis=1)
        repack(places, rows, scr, (keep, send))


def store_rows(ref, value, step, steps):
    for s in range(steps):

        @pl.when(step == s)
        def _(s=s):
            for i in range(PER):
                at = (s * PER + i) * SEQ
                ref[at : at + SEQ, :] = value[i * PAD : i * PAD + SEQ]


def input_grad_kernel(cuts, *refs):
    *pieces, w_ref, x_ref, mg_ref, gain_ref, out_ref, w_turned, grad = refs
    step = pl.program_id(0)

    @pl.when(step == 0)
    def _():
        w_turned[...] = w_ref[...].T

    at = 0
    for ref, count in zip(pieces, cuts, strict=True):

        @pl.when((step >= at) & (step < at + count))
        def _(ref=ref):
            grad[...] = tall(ref)

        at += count
    xhat, rstd = normalize(tall(x_ref).astype(F32))
    back = dot(grad[...], w_turned[...])
    dx = tall(mg_ref) + norm_back(back, xhat, rstd, gain_ref[0:1, :])
    store_rows(out_ref, dx, step, sum(cuts))


def layer_out_kernel(blocks, hid_ref, fc2_ref, mid_ref, out_ref, w_turned, all_rows):
    step = pl.program_id(0)

    @pl.when(step == 0)
    def _():
        w_turned[...] = fc2_ref[...].T

    y = tall(mid_ref) + dot(tall(hid_ref), w_turned[...])
    store_rows(all_rows, y, step, blocks)

    @pl.when(step == blocks - 1)
    def _():
        out_ref[...] = all_rows[...].astype(BF16)


def finish_first_kernel(mine, got, gain_ref, gain_grad, qkv_grad):
    total = mine[0].astype(F32) + got[0].astype(F32)
    for c in range(3):
        qkv_grad[c, :, 0:128] = total[:, c * 128 : c * 128 + 128]
        qkv_grad[c, :, 128:192] = total[:, 384 + c * HD : 448 + c * HD]
    gain_grad[...] = line(total[:, 576:577]) / gain_ref[...].astype(BF16).astype(F32)


def finish_rest_kernel(fs, mine, got, gain_ref, gain_grad, out_grad, fc1_grad, fc2_grad):
    total = mine[0].astype(F32) + got[0].astype(F32)
    out_grad[...] = total[:, :192]
    fc1_grad[...] = total[:, 256 : 256 + fs]
    fc2_grad[...] = total[:, 256 + fs :]
    gain_grad[...] = line(total[:, 192:193]) / gain_ref[...].astype(BF16).astype(F32)


def whole(*shape):
    return pl.BlockSpec(shape, lambda *i: (0,) * len(shape))


def part(first, count, *shape):
    return pl.BlockSpec((PER,) + shape, lambda i: (first + jnp.minimum(i, count - 1),) + (0,) * len(shape))


def late(first, count, *shape):
    return pl.BlockSpec((PER,) + shape, lambda i: (jnp.clip(i - first, 0, count - 1),) + (0,) * len(shape))


def call(kernel, grid, ins, outs, scratch, args, mflops=0, kbytes=0):
    return pl.pallas_call(
        kernel,
        grid=(grid,) if grid else (),
        in_specs=ins,
        out_specs=[spec for spec, _ in outs],
        out_shape=[shape for _, shape in outs],
        scratch_shapes=scratch,
        compiler_params=pltpu.CompilerParams(vmem_limit_bytes=VMEM_LIMIT),
        cost_estimate=pl.CostEstimate(flops=mflops * 10**6, bytes_accessed=kbytes * 1000, transcendentals=0),
    )(*args)


def shape_of(*shape, dtype=BF16):
    return jax.ShapeDtypeStruct(shape, dtype)


def padded(v, images):
    return jnp.pad(v.reshape(images, SEQ, D), ((0, 0), (0, PAD - SEQ), (0, 0)))


def local(sizes, tokens, ln1_gain, qkv_weight, out_weight, ln2_gain, fc1_weight, fc2_weight, out_grad):
    return layer(sizes, tokens, ln1_gain, qkv_weight, out_weight, ln2_gain, fc1_weight, fc2_weight, out_grad)


def layer(sizes, tokens, ln1_gain, qkv_weight, out_weight, ln2_gain, fc1_weight, fc2_weight, out_grad):
    stages = stage_bits(sizes["wide"])
    stages2 = stages[:-3] + [stages[-2], stages[-3], stages[-1]]
    places, places2 = relative(stages), relative(stages2)
    n = len(places)
    rows = own_rows = qkv_weight.shape[0]
    images = tokens.shape[0] // SEQ
    blocks = images // PER
    fs = fc1_weight.shape[1]
    ff = 2 * fs
    rc = 256 + 2 * fs
    big = images * PAD
    gain1, gain2 = ln1_gain.reshape(1, rows), ln2_gain.reshape(1, rows)

    first, rest = call(
        pack_kernel,
        0,
        [whole(3, rows, 192), whole(1, rows), whole(1, rows), whole(rows, 192), whole(rows, fs), whole(rows, fs)],
        [(whole(1, rows, QC), shape_of(1, rows, QC)), (whole(1, rows, rc), shape_of(1, rows, rc))],
        [],
        (qkv_weight.transpose(1, 0, 2), gain1, gain2, out_weight.T, fc1_weight, fc2_weight.T),
    )
    first_all = gather(first, stages, sizes)
    rest_all = gather(rest, stages, sizes)
    if rows % 8 != 0:
        n, rows = 16, 48
        first_all, rest_all = (
            jnp.split(in_order(places, jnp.concatenate(v, axis=0)), 4) for v in (first_all, rest_all)
        )

    x = padded(tokens, images)
    og = padded(out_grad, images)

    def row(*shape):
        return part(0, blocks, *shape)

    qkv, probs, heads, n1, w_qkv, gain = call(
        functools.partial(attend_kernel, places, rows),
        blocks,
        [whole(n // 4, rows, QC)] * 4 + [row(PAD, D)],
        [
            (row(PAD, 3 * D), shape_of(images, PAD, 3 * D)),
            (row(6, PAD, PAD), shape_of(images, 6, PAD, PAD)),
            (row(PAD, D), shape_of(images, PAD, D)),
            (row(PAD, D), shape_of(images, PAD, D)),
            (whole(D, 3 * D), shape_of(D, 3 * D)),
            (whole(8, D), shape_of(8, D, dtype=F32)),
        ],
        [pltpu.VMEM((2, D, QC), F32)],
        (*first_all, x),
        8000,
        20000,
    )
    wide1, wide2 = 256 + fs, fs
    middle, hid, mg, hg, fc2_t, keep1, send1, keep2, send2 = call(
        functools.partial(mlp_kernel, places, places2, rows, blocks, fs),
        blocks + 1,
        [whole(n // 4, rows, rc)] * 4 + [row(PAD, D), row(PAD, D), row(PAD, D), whole(8, D)],
        [
            (row(PAD, D), shape_of(images, PAD, D, dtype=F32)),
            (row(PAD, ff), shape_of(images, PAD, ff)),
            (row(PAD, D), shape_of(images, PAD, D, dtype=F32)),
            (row(PAD, D), shape_of(images, PAD, D)),
            (whole(D, ff), shape_of(D, ff)),
        ]
        + [(whole(n // 2, rows, w), shape_of(n // 2, rows, w)) for w in (wide1, wide1, wide2, wide2)],
        [
            pltpu.VMEM((2, D, rc), F32),
            pltpu.VMEM((D, D), BF16),
            pltpu.VMEM((D, D), BF16),
            pltpu.VMEM((D, ff), BF16),
            pltpu.VMEM((ff, D), BF16),
            pltpu.VMEM((big, D), BF16),
            pltpu.VMEM((big, ff), BF16),
            pltpu.VMEM((big, ff), BF16),
            pltpu.VMEM((big, D), BF16),
            pltpu.VMEM((big, D), BF16),
            pltpu.VMEM((big, D), BF16),
        ],
        (*rest_all, x, og, heads, gain),
        14000,
        30000,
    )

    if rows != own_rows:
        keep1, send1 = jnp.split(out_of_order(places, jnp.concatenate([keep1, send1], axis=0), own_rows), 2)
        keep2, send2 = jnp.split(out_of_order(places2, jnp.concatenate([keep2, send2], axis=0), own_rows), 2)
    back, back2 = stages[::-1], stages2[::-1]
    for s in range(3):
        keep1, send1 = half_sum(keep1, send1, back[s], sizes)
        keep2, send2 = half_sum(keep2, send2, back2[s], sizes)
    keep = jnp.concatenate([keep1, keep2], axis=2)
    send = jnp.concatenate([send1, send2], axis=2)
    for s in range(3, len(back) - 1):
        keep, send = half_sum(keep, send, back[s], sizes)
    got = swap(send, back[-1], sizes)
    ln2_grad, out_wgrad, fc1_grad, fc2_grad = call(
        functools.partial(finish_rest_kernel, fs),
        0,
        [whole(1, own_rows, rc)] * 2 + [whole(1, own_rows)],
        [
            (whole(1, own_rows), shape_of(1, own_rows, dtype=F32)),
            (whole(own_rows, 192), shape_of(own_rows, 192, dtype=F32)),
            (whole(own_rows, fs), shape_of(own_rows, fs, dtype=F32)),
            (whole(own_rows, fs), shape_of(own_rows, fs, dtype=F32)),
        ],
        [],
        (keep, got, gain2),
    )

    cuts = (1, blocks - 2, 1)
    pieces = []
    at = 0
    for count in cuts[:-1]:
        pieces += call(
            attend_back_kernel,
            count,
            [part(at, count, *s) for s in ((PAD, 3 * D), (6, PAD, PAD), (PAD, D))],
            [(part(0, count, PAD, 3 * D), shape_of(count * PER, PAD, 3 * D))],
            [],
            (qkv, probs, hg),
            1800 * count,
            4000 * count,
        )
        at += count
    left = cuts[-1]
    last, keep, send = call(
        functools.partial(attend_last_kernel, places, rows, left),
        left + 1,
        [part(at, left, *s) for s in ((PAD, 3 * D), (6, PAD, PAD), (PAD, D))]
        + [whole(images, PAD, D), whole(D, 3 * D)]
        + [whole(count * PER, PAD, 3 * D) for count in cuts[:-1]],
        [(part(0, left, PAD, 3 * D), shape_of(left * PER, PAD, 3 * D))]
        + [(whole(n // 2, rows, QC), shape_of(n // 2, rows, QC))] * 2,
        [pltpu.VMEM((2, D, QC), F32), pltpu.VMEM((big, 3 * D), BF16)],
        (qkv, probs, hg, n1, w_qkv, *pieces),
        3500,
        8000,
    )
    pieces.append(last)
    starts = [sum(cuts[:c]) for c in range(len(cuts))]
    (dx,) = call(
        functools.partial(input_grad_kernel, cuts),
        blocks,
        [late(at, count, PAD, 3 * D) for at, count in zip(starts, cuts, strict=True)]
        + [whole(D, 3 * D), row(PAD, D), row(PAD, D), whole(8, D)],
        [(whole(images * SEQ, D), shape_of(images * SEQ, D, dtype=F32))],
        [pltpu.VMEM((3 * D, D), BF16), pltpu.VMEM((PER * PAD, 3 * D), BF16)],
        (*pieces, w_qkv, x, mg, gain),
        2000,
        10000,
    )
    (y,) = call(
        functools.partial(layer_out_kernel, blocks),
        blocks,
        [row(PAD, ff), whole(D, ff), row(PAD, D)],
        [(whole(images * SEQ, D), shape_of(images * SEQ, D))],
        [pltpu.VMEM((ff, D), BF16), pltpu.VMEM((images * SEQ, D), F32)],
        (hid, fc2_t, middle),
        2000,
        10000,
    )

    if rows != own_rows:
        keep, send = jnp.split(out_of_order(places, jnp.concatenate([keep, send], axis=0), own_rows), 2)
    for stage in back[:-1]:
        keep, send = half_sum(keep, send, stage, sizes)
    got = swap(send, back[-1], sizes)
    ln1_grad, qkv_grad = call(
        finish_first_kernel,
        0,
        [whole(1, own_rows, QC)] * 2 + [whole(1, own_rows)],
        [
            (whole(1, own_rows), shape_of(1, own_rows, dtype=F32)),
            (whole(3, own_rows, 192), shape_of(3, own_rows, 192, dtype=F32)),
        ],
        [],
        (keep, got, gain1),
    )
    return (
        y,
        dx,
        ln1_grad.reshape(own_rows),
        qkv_grad.transpose(1, 0, 2),
        out_wgrad.T,
        ln2_grad.reshape(own_rows),
        fc1_grad,
        fc2_grad.T,
    )


def solution(mesh):
    rows = P(("wide", "tensor"), None)
    weights = (
        P("wide"),
        P("wide", None, "tensor"),
        P("tensor", "wide"),
        P("wide"),
        P("wide", "tensor"),
        P("tensor", "wide"),
    )
    return jax.shard_map(
        functools.partial(local, dict(mesh.shape)),
        mesh=mesh,
        in_specs=(rows, *weights, rows),
        out_specs=(rows, rows, *weights),
        check_vma=False,
    )
```

```python
import functools

import jax
import jax.numpy as jnp
from jax import lax
from jax.experimental import pallas as pl
from jax.experimental.pallas import tpu as pltpu
from jax.sharding import PartitionSpec as P

HD = 64
SEQ = 197
PAD = 208
PER = 2
CUT = 192
D = 384
QC = 640
F32 = jnp.float32
BF16 = jnp.bfloat16
NT = (((1,), (1,)), ((), ()))
GELU_C = 0.7978845608028654
VMEM_LIMIT = 60 * 1024 * 1024


def dot(a, b, dims=(((1,), (0,)), ((), ()))):
    return lax.dot_general(a, b, dims, preferred_element_type=F32)


def stage_bits(wide):
    bits = [("wide", 1 << k) for k in range(1, wide.bit_length() - 1)]
    bits = bits[:0:-1] + bits[:1]
    return bits + [("tensor", 1), ("wide", 1)]


def relative(stages):
    places = [(0, 0)]
    for axis, bit in stages:
        places = places + [(w ^ bit, t) if axis == "wide" else (w, t ^ bit) for w, t in places]
    return places


def swap(value, stage, sizes):
    axis, bit = stage
    return lax.ppermute(value, axis, [(i, i ^ bit) for i in range(sizes[axis])])


def gather(block, stages, sizes):
    held = block
    for stage in stages[:-2]:
        got = swap(held, stage, sizes)
        held = jnp.concatenate([held, got], axis=0)
    got = swap(held, stages[-2], sizes)
    return [held, got, swap(held, stages[-1], sizes), swap(got, stages[-1], sizes)]


def half_sum(keep, send, stage, sizes):
    got = swap(send, stage, sizes)
    total = (keep.astype(F32) + got.astype(F32)).astype(BF16)
    half = total.shape[0] // 2
    return total[:half], total[half:]


def in_order(places, held):
    me_w, me_t = lax.axis_index("wide"), lax.axis_index("tensor")
    at = {place: p for p, place in enumerate(places)}
    wide = len(places) // 2
    table = jnp.array([[at[w, t] for w in range(wide)] for t in range(2)], jnp.int32)
    order = table[me_t ^ jnp.arange(2)[:, None], me_w ^ jnp.arange(wide)[None, :]]
    return held[order.reshape(-1)].reshape(16, 48, held.shape[2])


def out_of_order(places, blocks, rows):
    me_w, me_t = lax.axis_index("wide"), lax.axis_index("tensor")
    wide = len(places) // 2
    order = jnp.array([w for w, _ in places], jnp.int32) ^ me_w
    order += wide * (jnp.array([t for _, t in places], jnp.int32) ^ me_t)
    return blocks.reshape(len(places), rows, blocks.shape[2])[order]


def rows_of(places, rows):
    if rows == 48:
        me_w, me_t = 0, 0
        places = [(w, t) for t in range(2) for w in range(8)]
    else:
        me_w, me_t = lax.axis_index("wide"), lax.axis_index("tensor")
    for p, (w, t) in enumerate(places):
        yield p, me_t ^ t, pl.ds(pl.multiple_of((me_w ^ w) * rows, 8), rows)


def unpack(places, rows, pieces, scr, at=0):
    size = len(pieces[0])
    width = pieces[0].shape[-1]
    for p, t, where in rows_of(places, rows):
        scr[t, where, at : at + width] = pieces[p // size][p % size].astype(F32)


def repack(places, rows, scr, pieces, at=0):
    size = len(pieces[0])
    width = pieces[0].shape[-1]
    for p, t, where in rows_of(places, rows):
        pieces[p // size][p % size] = scr[t, where, at : at + width].astype(BF16)


def normalize(v):
    center = v - jnp.mean(v, axis=-1, keepdims=True)
    rstd = lax.rsqrt(jnp.mean(center * center, axis=-1, keepdims=True) + 1e-06)
    return center * rstd, rstd


def norm_back(grad, xhat, rstd, gain):
    g = grad * gain
    return rstd * (
        g
        - jnp.mean(g, axis=-1, keepdims=True)
        - xhat * jnp.mean(g * xhat, axis=-1, keepdims=True)
    )


def low_lanes():
    return lax.broadcasted_iota(jnp.int32, (PAD, 128), 1) < HD


def pick(value, low, side):
    zero = jnp.zeros_like(value)
    return jnp.where(low, value, zero) if side == 0 else jnp.where(low, zero, value)


def lanes(kind, c):
    return slice((3 * c + kind) * 128, (3 * c + kind) * 128 + 128)


def tall(ref):
    return ref[...].reshape(PER * PAD, ref.shape[-1])


def column(row):
    n = row.shape[1]
    own = lax.broadcasted_iota(jnp.int32, (n, n), 0) == lax.broadcasted_iota(jnp.int32, (n, n), 1)
    return jnp.sum(jnp.where(own, jnp.broadcast_to(row, (n, n)), 0.0), axis=1, keepdims=True)


def line(col):
    n = col.shape[0]
    own = lax.broadcasted_iota(jnp.int32, (n, n), 0) == lax.broadcasted_iota(jnp.int32, (n, n), 1)
    return jnp.sum(jnp.where(own, jnp.broadcast_to(col, (n, n)), 0.0), axis=0, keepdims=True)


def pack_kernel(qkv, gain1, gain2, out, fc1, fc2, first, rest):
    rows = out.shape[0]
    fs = fc1.shape[1]
    lane = lax.broadcasted_iota(jnp.int32, (rows, HD), 1)
    gains = jnp.where(lane == 0, column(gain1[...]), jnp.where(lane == 1, column(gain2[...]), 0.0))
    for c in range(3):
        first[0, :, c * 128 : c * 128 + 128] = qkv[c, :, 0:128]
    single = [qkv[c, :, 128:192].astype(F32) for c in range(3)]
    first[0, :, 384:512] = jnp.concatenate(single[:2], axis=1).astype(BF16)
    first[0, :, 512:640] = jnp.concatenate([single[2], gains], axis=1).astype(BF16)
    rest[0, :, 0:128] = out[:, 0:128]
    pad = jnp.zeros((rows, HD), F32)
    rest[0, :, 128:256] = jnp.concatenate([out[:, 128:192].astype(F32), pad], axis=1).astype(BF16)
    rest[0, :, 256 : 256 + fs] = fc1[...]
    rest[0, :, 256 + fs :] = fc2[...]


def attend_kernel(places, rows, p0, p1, p2, p3, x_ref, qkv_ref, probs_ref, heads_ref, n1_ref, w_ref, gain_ref, scr):
    @pl.when(pl.program_id(0) == 0)
    def _():
        unpack(places, rows, (p0, p1, p2, p3), scr)
        for t in range(2):
            w_ref[:, t * D : t * D + D] = scr[t, :, 0:D].astype(BF16)
        for kind in range(3):
            one = slice(D + kind * HD, D + kind * HD + HD)
            last = jnp.concatenate([scr[0, :, one], scr[1, :, one]], axis=1)
            w_ref[:, lanes(kind, 2)] = last.astype(BF16)
        turned = scr[0, :, 512:640].T
        gain_ref[...] = turned[HD : HD + 8, :]

    xhat, _ = normalize(tall(x_ref).astype(F32))
    n1 = (xhat * gain_ref[0:1, :]).astype(BF16)
    n1_ref[...] = n1.reshape(PER, PAD, D)
    low = low_lanes()
    tail_ok = lax.broadcasted_iota(jnp.int32, (PAD - CUT, PAD), 0) < SEQ - CUT

    def project(c):
        for b in {0: (0, 1), 1: (2,), 2: (3, 4)}[c]:
            at = slice(b * 256, min(b * 256 + 256, 3 * D))
            value = dot(n1, w_ref[:, at])
            for piece in range((at.stop - at.start) // 128):
                kind = (b * 2 + piece) % 3
                here = value[:, piece * 128 : piece * 128 + 128]
                if kind == 0:
                    here = here * (HD**-0.5)
                span = slice(at.start + piece * 128, at.start + piece * 128 + 128)
                qkv_ref[:, :, span] = here.astype(BF16).reshape(PER, PAD, 128)

    def enter(i, c):
        q, k, v = (qkv_ref[i, :, lanes(kind, c)] for kind in range(3))
        return [dot(pick(k, low, side), q, NT) for side in range(2)], v.T

    units = [(i, c) for c in range(3) for i in range(PER)]
    project(0)
    ahead = enter(*units[0])
    for j, (i, c) in enumerate(units):
        all_scores, v_turned = ahead
        if j + 1 < len(units):
            if i == 0 and c < 2:
                project(c + 1)
            ahead = enter(*units[j + 1])
        parts = []
        for side in range(2):
            scores = all_scores[side]
            scores = jnp.concatenate([scores[:CUT], jnp.where(tail_ok, scores[CUT:], -1e30)], axis=0)
            expon = jnp.exp(scores - jnp.max(scores, axis=0, keepdims=True))
            probs = expon * (1.0 / jnp.sum(expon, axis=0, keepdims=True))
            probs = probs.astype(BF16)
            probs_ref[i, 2 * c + side] = probs
            parts.append(dot(v_turned[side * HD : side * HD + HD, :], probs))
        heads_ref[i, :, c * 128 : c * 128 + 128] = jnp.concatenate(parts, axis=0).T.astype(BF16)


def mlp_kernel(
    places, places2, rows, blocks, fs, p0, p1, p2, p3, x_ref, og_ref, h_ref, gain_ref,
    mid_ref, hid_ref, mg_ref, hg_ref, fc2_ref, keep1, send1, keep2, send2,
    scr, w_out, w_back, w_fc1, w_fc1_turned, n2_all, pg_all, hid_all, og_all, ml_all, h_all,
):
    step = pl.program_id(0)

    @pl.when(step == 0)
    def _():
        unpack(places, rows, (p0, p1, p2, p3), scr)
        last = jnp.concatenate([scr[0, :, 128:192], scr[1, :, 128:192]], axis=1)
        for b, value in enumerate((scr[0, :, 0:128], scr[1, :, 0:128], last)):
            w_back[:, b * 128 : b * 128 + 128] = value.astype(BF16)
            w_out[b * 128 : b * 128 + 128, :] = value.T.astype(BF16)
        for t in range(2):
            at = slice(t * fs, t * fs + fs)
            w_fc1[:, at] = scr[t, :, 256 : 256 + fs].astype(BF16)
            w_fc1_turned[at, :] = scr[t, :, 256 : 256 + fs].T.astype(BF16)
            fc2_ref[:, at] = scr[t, :, 256 + fs :].astype(BF16)

    @pl.when(step < blocks)
    def _():
        size = PER * PAD
        at = pl.ds(pl.multiple_of(step * size, size), size)
        gain = gain_ref[1:2, :]
        h = tall(h_ref)
        og = tall(og_ref)
        h_all[at, :] = h
        og_all[at, :] = og
        middle = tall(x_ref).astype(F32) + dot(h, w_out[...])
        mid_ref[...] = middle.reshape(PER, PAD, D)
        xhat, rstd = normalize(middle)
        n2 = (xhat * gain).astype(BF16)
        n2_all[at, :] = n2
        width = 256
        back = None
        count = 2 * fs // width
        ahead = dot(n2, w_fc1[:, :width]), dot(og, fc2_ref[:, :width])
        for c in range(count):
            cols = slice(c * width, c * width + width)
            u, dh = ahead
            if c + 1 < count:
                after = slice(c * width + width, c * width + 2 * width)
                ahead = dot(n2, w_fc1[:, after]), dot(og, fc2_ref[:, after])
            square = u * u
            bent = jnp.tanh(u * (GELU_C + (GELU_C * 0.044715) * square))
            plus = 0.5 + 0.5 * bent
            full = u * plus
            hid = full.astype(BF16)
            hid_ref[:, :, cols] = hid.reshape(PER, PAD, width)
            hid_all[at, cols] = hid
            slope = plus + full * (1.0 - plus) * ((2.0 * GELU_C) + (GELU_C * 0.26829) * square)
            pg = (dh * slope).astype(BF16)
            pg_all[at, cols] = pg
            part = dot(pg, w_fc1_turned[cols, :])
            back = part if back is None else back + part
        mg = og.astype(F32) + norm_back(back, xhat, rstd, gain)
        mg_ref[...] = mg.reshape(PER, PAD, D)
        ml = mg.astype(BF16)
        ml_all[at, :] = ml
        hg_ref[...] = dot(ml, w_back[...]).astype(BF16).reshape(PER, PAD, D)

    @pl.when(step == blocks)
    def _():
        turned = n2_all[...].T
        row_sum = jnp.zeros((D, 1), F32)
        chunk = fs // 3
        for t in range(2):
            for c in range(3):
                cols = slice(t * fs + c * chunk, t * fs + c * chunk + chunk)
                grad = dot(turned, pg_all[:, cols])
                scr[t, :, 256 + c * chunk : 256 + c * chunk + chunk] = grad
                row_sum += jnp.sum(grad * w_fc1[:, cols].astype(F32), axis=1, keepdims=True)
        turned = og_all[...].T
        for t in range(2):
            for c in range(3):
                cols = slice(t * fs + c * chunk, t * fs + c * chunk + chunk)
                scr[t, :, 256 + fs + c * chunk : 256 + fs + c * chunk + chunk] = dot(turned, hid_all[:, cols])
        grad = dot(ml_all[...].T, h_all[...])
        scr[0, :, 0:128] = grad[:, 0:128]
        scr[1, :, 0:128] = grad[:, 128:256]
        gain = jnp.broadcast_to(row_sum, (D, HD))
        scr[0, :, 128:256] = jnp.concatenate([grad[:, 256 : 256 + HD], gain], axis=1)
        scr[1, :, 128:256] = jnp.concatenate([grad[:, 256 + HD : 384], gain], axis=1)
        repack(places, rows, scr, (keep1, send1))
        repack(places2, rows, scr, (keep2, send2), 256 + fs)


def attend_back(qkv_ref, probs_ref, hg_ref, grad_ref, grad_all, at):
    low = low_lanes()
    units = [(i, c) for i in range(PER) for c in range(3)]

    def enter(i, c):
        v, do = qkv_ref[i, :, lanes(2, c)], hg_ref[i, :, c * 128 : c * 128 + 128]
        return [dot(pick(v, low, side), do, NT) for side in range(2)]

    ahead = enter(*units[0])
    for j, (i, c) in enumerate(units):
        grads = ahead
        if j + 1 < len(units):
            ahead = enter(*units[j + 1])
        low_probs = [probs_ref[i, 2 * c + side] for side in range(2)]
        ds = []
        for side in range(2):
            probs = low_probs[side].astype(F32)
            weighted = probs * grads[side]
            ds.append((weighted - probs * jnp.sum(weighted, axis=0, keepdims=True)).astype(BF16))
        q, k = qkv_ref[i, :, lanes(0, c)], qkv_ref[i, :, lanes(1, c)]
        do = hg_ref[i, :, c * 128 : c * 128 + 128]
        k_turned = k.T
        dv = [dot(p, do) for p in low_probs]
        dk = [dot(d, q) for d in ds]
        dq = [dot(k_turned[side * HD : side * HD + HD, :], ds[side]) for side in range(2)]
        for kind, value in (
            (0, jnp.concatenate(dq, axis=0).T * (HD**-0.5)),
            (1, jnp.where(low, dk[0], dk[1])),
            (2, jnp.where(low, dv[0], dv[1])),
        ):
            value = value.astype(BF16)
            grad_ref[i, :, lanes(kind, c)] = value
            if grad_all is not None:
                grad_all[pl.ds(pl.multiple_of(at + i * PAD, PAD), PAD), lanes(kind, c)] = value


def attend_back_kernel(qkv_ref, probs_ref, hg_ref, grad_ref):
    attend_back(qkv_ref, probs_ref, hg_ref, grad_ref, None, 0)


def attend_last_kernel(
    places, rows, blocks, qkv_ref, probs_ref, hg_ref, n1_ref, w_ref, *refs
):
    *earlier, grad_ref, keep, send, scr, grad_all = refs
    step = pl.program_id(0)
    early = sum(ref.shape[0] for ref in earlier) * PAD

    @pl.when(step == 0)
    def _():
        at = 0
        for ref in earlier:
            size = ref.shape[0] * PAD
            grad_all[at : at + size, :] = ref[...].reshape(size, 3 * D)
            at += size

    @pl.when(step < blocks)
    def _():
        attend_back(qkv_ref, probs_ref, hg_ref, grad_ref, grad_all, early + step * PER * PAD)

    @pl.when(step == blocks)
    def _():
        turned = n1_ref[...].reshape(-1, D).T
        row_sum = jnp.zeros((D, 1), F32)
        singles = [None] * 3
        for b in (8, 6, 0, 2, 4):
            blocks_here = range(b, min(b + 2, 9))
            span = slice(b * 128, blocks_here.stop * 128)
            grad = dot(turned, grad_all[:, span])
            row_sum += jnp.sum(grad * w_ref[:, span].astype(F32), axis=1, keepdims=True)
            for at in blocks_here:
                here = grad[:, (at - b) * 128 : (at - b) * 128 + 128]
                if at < 6:
                    scr[at // 3, :, at % 3 * 128 : at % 3 * 128 + 128] = here
                else:
                    singles[at - 6] = here
            if b == 6:
                for t in range(2):
                    own = [s[:, t * HD : t * HD + HD] for s in singles]
                    scr[t, :, 384:512] = jnp.concatenate(own[:2], axis=1)
                    scr[t, :, 512 : 512 + HD] = own[2]
        scr[:, :, 512 + HD : 640] = jnp.broadcast_to(row_sum[None], (2, D, HD))
        repack(places, rows, scr, (keep, send))


def store_rows(ref, value, step, steps):
    for s in range(steps):

        @pl.when(step == s)
        def _(s=s):
            for i in range(PER):
                at = (s * PER + i) * SEQ
                ref[at : at + SEQ, :] = value[i * PAD : i * PAD + SEQ]


def input_grad_kernel(cuts, *refs):
    *pieces, w_ref, x_ref, mg_ref, gain_ref, out_ref, w_turned, grad = refs
    step = pl.program_id(0)

    @pl.when(step == 0)
    def _():
        w_turned[...] = w_ref[...].T

    at = 0
    for ref, count in zip(pieces, cuts, strict=True):

        @pl.when((step >= at) & (step < at + count))
        def _(ref=ref):
            grad[...] = tall(ref)

        at += count
    xhat, rstd = normalize(tall(x_ref).astype(F32))
    back = dot(grad[...], w_turned[...])
    dx = tall(mg_ref) + norm_back(back, xhat, rstd, gain_ref[0:1, :])
    store_rows(out_ref, dx, step, sum(cuts))


def layer_out_kernel(blocks, hid_ref, fc2_ref, mid_ref, out_ref, w_turned, all_rows):
    step = pl.program_id(0)

    @pl.when(step == 0)
    def _():
        w_turned[...] = fc2_ref[...].T

    y = tall(mid_ref) + dot(tall(hid_ref), w_turned[...])
    store_rows(all_rows, y, step, blocks)

    @pl.when(step == blocks - 1)
    def _():
        out_ref[...] = all_rows[...].astype(BF16)


def finish_first_kernel(mine, got, gain_ref, gain_grad, qkv_grad):
    total = mine[0].astype(F32) + got[0].astype(F32)
    for c in range(3):
        qkv_grad[c, :, 0:128] = total[:, c * 128 : c * 128 + 128]
        qkv_grad[c, :, 128:192] = total[:, 384 + c * HD : 448 + c * HD]
    gain_grad[...] = line(total[:, 576:577]) / gain_ref[...].astype(BF16).astype(F32)


def finish_rest_kernel(fs, mine, got, gain_ref, gain_grad, out_grad, fc1_grad, fc2_grad):
    total = mine[0].astype(F32) + got[0].astype(F32)
    out_grad[...] = total[:, :192]
    fc1_grad[...] = total[:, 256 : 256 + fs]
    fc2_grad[...] = total[:, 256 + fs :]
    gain_grad[...] = line(total[:, 192:193]) / gain_ref[...].astype(BF16).astype(F32)


def whole(*shape):
    return pl.BlockSpec(shape, lambda *i: (0,) * len(shape))


def part(first, count, *shape):
    return pl.BlockSpec((PER,) + shape, lambda i: (first + jnp.minimum(i, count - 1),) + (0,) * len(shape))


def late(first, count, *shape):
    return pl.BlockSpec((PER,) + shape, lambda i: (jnp.clip(i - first, 0, count - 1),) + (0,) * len(shape))


def call(kernel, grid, ins, outs, scratch, args, mflops=0, kbytes=0):
    return pl.pallas_call(
        kernel,
        grid=(grid,) if grid else (),
        in_specs=ins,
        out_specs=[spec for spec, _ in outs],
        out_shape=[shape for _, shape in outs],
        scratch_shapes=scratch,
        compiler_params=pltpu.CompilerParams(vmem_limit_bytes=VMEM_LIMIT),
        cost_estimate=pl.CostEstimate(flops=mflops * 10**6, bytes_accessed=kbytes * 1000, transcendentals=0),
    )(*args)


def shape_of(*shape, dtype=BF16):
    return jax.ShapeDtypeStruct(shape, dtype)


def padded(v, images):
    return jnp.pad(v.reshape(images, SEQ, D), ((0, 0), (0, PAD - SEQ), (0, 0)))


def local(sizes, tokens, ln1_gain, qkv_weight, out_weight, ln2_gain, fc1_weight, fc2_weight, out_grad):
    return layer(sizes, tokens, ln1_gain, qkv_weight, out_weight, ln2_gain, fc1_weight, fc2_weight, out_grad)


def layer(sizes, tokens, ln1_gain, qkv_weight, out_weight, ln2_gain, fc1_weight, fc2_weight, out_grad):
    stages = stage_bits(sizes["wide"])
    stages2 = stages[:-3] + [stages[-2], stages[-3], stages[-1]]
    places, places2 = relative(stages), relative(stages2)
    n = len(places)
    rows = own_rows = qkv_weight.shape[0]
    images = tokens.shape[0] // SEQ
    blocks = images // PER
    fs = fc1_weight.shape[1]
    ff = 2 * fs
    rc = 256 + 2 * fs
    big = images * PAD
    gain1, gain2 = ln1_gain.reshape(1, rows), ln2_gain.reshape(1, rows)

    first, rest = call(
        pack_kernel,
        0,
        [whole(3, rows, 192), whole(1, rows), whole(1, rows), whole(rows, 192), whole(rows, fs), whole(rows, fs)],
        [(whole(1, rows, QC), shape_of(1, rows, QC)), (whole(1, rows, rc), shape_of(1, rows, rc))],
        [],
        (qkv_weight.transpose(1, 0, 2), gain1, gain2, out_weight.T, fc1_weight, fc2_weight.T),
    )
    first_all = gather(first, stages, sizes)
    rest_all = gather(rest, stages, sizes)
    if rows % 8 != 0:
        n, rows = 16, 48
        first_all, rest_all = (
            jnp.split(in_order(places, jnp.concatenate(v, axis=0)), 4) for v in (first_all, rest_all)
        )

    x = padded(tokens, images)
    og = padded(out_grad, images)

    def row(*shape):
        return part(0, blocks, *shape)

    qkv, probs, heads, n1, w_qkv, gain = call(
        functools.partial(attend_kernel, places, rows),
        blocks,
        [whole(n // 4, rows, QC)] * 4 + [row(PAD, D)],
        [
            (row(PAD, 3 * D), shape_of(images, PAD, 3 * D)),
            (row(6, PAD, PAD), shape_of(images, 6, PAD, PAD)),
            (row(PAD, D), shape_of(images, PAD, D)),
            (row(PAD, D), shape_of(images, PAD, D)),
            (whole(D, 3 * D), shape_of(D, 3 * D)),
            (whole(8, D), shape_of(8, D, dtype=F32)),
        ],
        [pltpu.VMEM((2, D, QC), F32)],
        (*first_all, x),
        8000,
        20000,
    )
    wide1, wide2 = 256 + fs, fs
    middle, hid, mg, hg, fc2_t, keep1, send1, keep2, send2 = call(
        functools.partial(mlp_kernel, places, places2, rows, blocks, fs),
        blocks + 1,
        [whole(n // 4, rows, rc)] * 4 + [row(PAD, D), row(PAD, D), row(PAD, D), whole(8, D)],
        [
            (row(PAD, D), shape_of(images, PAD, D, dtype=F32)),
            (row(PAD, ff), shape_of(images, PAD, ff)),
            (row(PAD, D), shape_of(images, PAD, D, dtype=F32)),
            (row(PAD, D), shape_of(images, PAD, D)),
            (whole(D, ff), shape_of(D, ff)),
        ]
        + [(whole(n // 2, rows, w), shape_of(n // 2, rows, w)) for w in (wide1, wide1, wide2, wide2)],
        [
            pltpu.VMEM((2, D, rc), F32),
            pltpu.VMEM((D, D), BF16),
            pltpu.VMEM((D, D), BF16),
            pltpu.VMEM((D, ff), BF16),
            pltpu.VMEM((ff, D), BF16),
            pltpu.VMEM((big, D), BF16),
            pltpu.VMEM((big, ff), BF16),
            pltpu.VMEM((big, ff), BF16),
            pltpu.VMEM((big, D), BF16),
            pltpu.VMEM((big, D), BF16),
            pltpu.VMEM((big, D), BF16),
        ],
        (*rest_all, x, og, heads, gain),
        14000,
        30000,
    )

    if rows != own_rows:
        keep1, send1 = jnp.split(out_of_order(places, jnp.concatenate([keep1, send1], axis=0), own_rows), 2)
        keep2, send2 = jnp.split(out_of_order(places2, jnp.concatenate([keep2, send2], axis=0), own_rows), 2)
    back, back2 = stages[::-1], stages2[::-1]
    for s in range(3):
        keep1, send1 = half_sum(keep1, send1, back[s], sizes)
        keep2, send2 = half_sum(keep2, send2, back2[s], sizes)
    keep = jnp.concatenate([keep1, keep2], axis=2)
    send = jnp.concatenate([send1, send2], axis=2)
    for s in range(3, len(back) - 1):
        keep, send = half_sum(keep, send, back[s], sizes)
    got = swap(send, back[-1], sizes)
    ln2_grad, out_wgrad, fc1_grad, fc2_grad = call(
        functools.partial(finish_rest_kernel, fs),
        0,
        [whole(1, own_rows, rc)] * 2 + [whole(1, own_rows)],
        [
            (whole(1, own_rows), shape_of(1, own_rows, dtype=F32)),
            (whole(own_rows, 192), shape_of(own_rows, 192, dtype=F32)),
            (whole(own_rows, fs), shape_of(own_rows, fs, dtype=F32)),
            (whole(own_rows, fs), shape_of(own_rows, fs, dtype=F32)),
        ],
        [],
        (keep, got, gain2),
    )

    cuts = (1, blocks - 2, 1)
    pieces = []
    at = 0
    for count in cuts[:-1]:
        pieces += call(
            attend_back_kernel,
            count,
            [part(at, count, *s) for s in ((PAD, 3 * D), (6, PAD, PAD), (PAD, D))],
            [(part(0, count, PAD, 3 * D), shape_of(count * PER, PAD, 3 * D))],
            [],
            (qkv, probs, hg),
            1800 * count,
            4000 * count,
        )
        at += count
    left = cuts[-1]
    last, keep, send = call(
        functools.partial(attend_last_kernel, places, rows, left),
        left + 1,
        [part(at, left, *s) for s in ((PAD, 3 * D), (6, PAD, PAD), (PAD, D))]
        + [whole(images, PAD, D), whole(D, 3 * D)]
        + [whole(count * PER, PAD, 3 * D) for count in cuts[:-1]],
        [(part(0, left, PAD, 3 * D), shape_of(left * PER, PAD, 3 * D))]
        + [(whole(n // 2, rows, QC), shape_of(n // 2, rows, QC))] * 2,
        [pltpu.VMEM((2, D, QC), F32), pltpu.VMEM((big, 3 * D), BF16)],
        (qkv, probs, hg, n1, w_qkv, *pieces),
        3500,
        8000,
    )
    pieces.append(last)
    starts = [sum(cuts[:c]) for c in range(len(cuts))]
    (dx,) = call(
        functools.partial(input_grad_kernel, cuts),
        blocks,
        [late(at, count, PAD, 3 * D) for at, count in zip(starts, cuts, strict=True)]
        + [whole(D, 3 * D), row(PAD, D), row(PAD, D), whole(8, D)],
        [(whole(images * SEQ, D), shape_of(images * SEQ, D, dtype=F32))],
        [pltpu.VMEM((3 * D, D), BF16), pltpu.VMEM((PER * PAD, 3 * D), BF16)],
        (*pieces, w_qkv, x, mg, gain),
        2000,
        10000,
    )
    (y,) = call(
        functools.partial(layer_out_kernel, blocks),
        blocks,
        [row(PAD, ff), whole(D, ff), row(PAD, D)],
        [(whole(images * SEQ, D), shape_of(images * SEQ, D))],
        [pltpu.VMEM((ff, D), BF16), pltpu.VMEM((images * SEQ, D), F32)],
        (hid, fc2_t, middle),
        2000,
        10000,
    )

    if rows != own_rows:
        keep, send = jnp.split(out_of_order(places, jnp.concatenate([keep, send], axis=0), own_rows), 2)
    for stage in back[:-1]:
        keep, send = half_sum(keep, send, stage, sizes)
    got = swap(send, back[-1], sizes)
    ln1_grad, qkv_grad = call(
        finish_first_kernel,
        0,
        [whole(1, own_rows, QC)] * 2 + [whole(1, own_rows)],
        [
            (whole(1, own_rows), shape_of(1, own_rows, dtype=F32)),
            (whole(3, own_rows, 192), shape_of(3, own_rows, 192, dtype=F32)),
        ],
        [],
        (keep, got, gain1),
    )
    return (
        y,
        dx,
        ln1_grad.reshape(own_rows),
        qkv_grad.transpose(1, 0, 2),
        out_wgrad.T,
        ln2_grad.reshape(own_rows),
        fc1_grad,
        fc2_grad.T,
    )


def solution(mesh):
    rows = P(("wide", "tensor"), None)
    weights = (
        P("wide"),
        P("wide", None, "tensor"),
        P("tensor", "wide"),
        P("wide"),
        P("wide", "tensor"),
        P("tensor", "wide"),
    )
    return jax.shard_map(
        functools.partial(local, dict(mesh.shape)),
        mesh=mesh,
        in_specs=(rows, *weights, rows),
        out_specs=(rows, rows, *weights),
        check_vma=False,
    )
```

```python
import functools

import jax
import jax.numpy as jnp
from jax import lax
from jax.experimental import pallas as pl
from jax.experimental.pallas import tpu as pltpu
from jax.sharding import PartitionSpec as P

HD = 64
SEQ = 197
PAD = 208
PER = 2
CUT = 192
WIDE = 512
LANES = 256
D = 384
QC = 640
F32 = jnp.float32
BF16 = jnp.bfloat16
NT = (((1,), (1,)), ((), ()))
GELU_C = 0.7978845608028654


def dot(a, b, dims=(((1,), (0,)), ((), ()))):
    return lax.dot_general(a, b, dims, preferred_element_type=F32)


def stage_bits(wide):
    bits = [("wide", 1 << k) for k in range(1, wide.bit_length() - 1)]
    bits = bits[:0:-1] + bits[:1]
    return bits + [("tensor", 1), ("wide", 1)]


def relative(stages):
    places = [(0, 0)]
    for axis, bit in stages:
        places = places + [(w ^ bit, t) if axis == "wide" else (w, t ^ bit) for w, t in places]
    return places


def swap(value, stage, sizes):
    axis, bit = stage
    return lax.ppermute(value, axis, [(i, i ^ bit) for i in range(sizes[axis])])


def gather(held, stages, sizes):
    for stage in stages[:-2]:
        held = grow(held, stage, sizes)
    got = swap(held, stages[-2], sizes)
    return [held, got, swap(held, stages[-1], sizes), swap(got, stages[-1], sizes)]


def grow(held, stage, sizes):
    got = swap(held, stage, sizes)
    return jnp.concatenate([held, got], axis=0)


def reduce_stage(total, stage, sizes):
    half = total.shape[0] // 2
    return add_got(total[:half], swap(total[half:], stage, sizes))


def add_got(keep, got):
    return (keep.astype(F32) + got.astype(F32)).astype(BF16)


def in_order(places, held):
    me_w, me_t = lax.axis_index("wide"), lax.axis_index("tensor")
    at = {place: p for p, place in enumerate(places)}
    wide = len(places) // 2
    table = jnp.array([[at[w, t] for w in range(wide)] for t in range(2)], jnp.int32)
    order = table[me_t ^ jnp.arange(2)[:, None], me_w ^ jnp.arange(wide)[None, :]]
    return held[order.reshape(-1)].reshape(16, 48, held.shape[2])


def out_of_order(places, blocks, rows):
    me_w, me_t = lax.axis_index("wide"), lax.axis_index("tensor")
    wide = len(places) // 2
    order = jnp.array([w for w, _ in places], jnp.int32) ^ me_w
    order += wide * (jnp.array([t for _, t in places], jnp.int32) ^ me_t)
    return blocks.reshape(len(places), rows, blocks.shape[2])[order]


def rows_of(places, rows):
    if rows == 48:
        me_w, me_t = 0, 0
        places = [(w, t) for t in range(2) for w in range(8)]
    else:
        me_w, me_t = lax.axis_index("wide"), lax.axis_index("tensor")
    for p, (w, t) in enumerate(places):
        yield p, me_t ^ t, pl.ds(pl.multiple_of((me_w ^ w) * rows, 8), rows)


def unpack(places, rows, pieces, scr, at=0):
    size = len(pieces[0])
    width = pieces[0].shape[-1]
    for p, t, where in rows_of(places, rows):
        scr[t, where, at : at + width] = pieces[p // size][p % size].astype(F32)


def repack(places, rows, scr, pieces, at=0):
    size = len(pieces[0])
    width = pieces[0].shape[-1]
    for p, t, where in rows_of(places, rows):
        pieces[p // size][p % size] = scr[t, where, at : at + width].astype(BF16)


def normalize(v):
    center = v - jnp.mean(v, axis=-1, keepdims=True)
    rstd = lax.rsqrt(jnp.mean(center * center, axis=-1, keepdims=True) + 1e-06)
    return center * rstd, rstd


def norm_back(grad, xhat, rstd, gain):
    g = grad * gain
    return rstd * (
        g
        - jnp.mean(g, axis=-1, keepdims=True)
        - xhat * jnp.mean(g * xhat, axis=-1, keepdims=True)
    )


def low_lanes():
    return lax.broadcasted_iota(jnp.int32, (PAD, 128), 1) < HD


def both_heads(value, low):
    zero = jnp.zeros_like(value)
    gap = jnp.zeros((LANES - PAD, 128), value.dtype)
    return jnp.concatenate([jnp.where(low, value, zero), gap, jnp.where(low, zero, value), gap], axis=0)


def own_heads(value):
    own = jnp.concatenate([value[:HD, :LANES], value[HD:, LANES:]], axis=0)
    return own.T[:PAD]


def lanes(kind, c):
    return slice((3 * c + kind) * 128, (3 * c + kind) * 128 + 128)


def tall(ref):
    return ref[...].reshape(PER * PAD, ref.shape[-1])


def column(row):
    n = row.shape[1]
    own = lax.broadcasted_iota(jnp.int32, (n, n), 0) == lax.broadcasted_iota(jnp.int32, (n, n), 1)
    return jnp.sum(jnp.where(own, jnp.broadcast_to(row, (n, n)), 0.0), axis=1, keepdims=True)


def line(col):
    n = col.shape[0]
    own = lax.broadcasted_iota(jnp.int32, (n, n), 0) == lax.broadcasted_iota(jnp.int32, (n, n), 1)
    return jnp.sum(jnp.where(own, jnp.broadcast_to(col, (n, n)), 0.0), axis=0, keepdims=True)


def pack_kernel(qkv, gain1, gain2, out, fc1, fc2, first, rest):
    rows = out.shape[0]
    fs = fc1.shape[1]
    lane = lax.broadcasted_iota(jnp.int32, (rows, HD), 1)
    gains = jnp.where(lane == 0, column(gain1[...]), jnp.where(lane == 1, column(gain2[...]), 0.0))
    for c in range(3):
        first[0, :, c * 128 : c * 128 + 128] = qkv[c, :, 0:128]
    single = [qkv[c, :, 128:192].astype(F32) for c in range(3)]
    first[0, :, 384:512] = jnp.concatenate(single[:2], axis=1).astype(BF16)
    first[0, :, 512:640] = jnp.concatenate([single[2], gains], axis=1).astype(BF16)
    rest[0, :, 0:128] = out[:, 0:128]
    pad = jnp.zeros((rows, HD), F32)
    rest[0, :, 128:256] = jnp.concatenate([out[:, 128:192].astype(F32), pad], axis=1).astype(BF16)
    rest[0, :, 256 : 256 + fs] = fc1[...]
    rest[0, :, 256 + fs :] = fc2[...]


def attend_kernel(places, rows, p0, p1, p2, p3, x_ref, qkv_ref, probs_ref, heads_ref, n1_ref, w_ref, gain_ref, scr):
    @pl.when(pl.program_id(0) == 0)
    def _():
        unpack(places, rows, (p0, p1, p2, p3), scr)
        for t in range(2):
            w_ref[:, t * D : t * D + D] = scr[t, :, 0:D].astype(BF16)
        for kind in range(3):
            one = slice(D + kind * HD, D + kind * HD + HD)
            last = jnp.concatenate([scr[0, :, one], scr[1, :, one]], axis=1)
            w_ref[:, lanes(kind, 2)] = last.astype(BF16)
        turned = scr[0, :, 512:640].T
        gain_ref[...] = turned[HD : HD + 8, :]

    xhat, _ = normalize(tall(x_ref).astype(F32))
    n1 = (xhat * gain_ref[0:1, :]).astype(BF16)
    n1_ref[...] = n1.reshape(PER, PAD, D)
    low = low_lanes()
    tail_ok = lax.broadcasted_iota(jnp.int32, (PAD - CUT, WIDE), 0) < SEQ - CUT

    def project(c):
        at = slice(c * WIDE, min(c * WIDE + WIDE, 3 * D))
        value = dot(n1, w_ref[:, at])
        for piece in range((at.stop - at.start) // 128):
            here = value[:, piece * 128 : piece * 128 + 128]
            if (c * 4 + piece) % 3 == 0:
                here = here * (HD**-0.5)
            span = slice(at.start + piece * 128, at.start + piece * 128 + 128)
            qkv_ref[:, :, span] = here.astype(BF16).reshape(PER, PAD, 128)

    def enter(i, c):
        q, k, v = (qkv_ref[i, :, lanes(kind, c)] for kind in range(3))
        return dot(k, both_heads(q, low), NT), v.T

    units = [(i, c) for c in range(3) for i in range(PER)]
    project(0)
    ahead = enter(*units[0])
    for j, (i, c) in enumerate(units):
        scores, v_turned = ahead
        if j + 1 < len(units):
            if i == 0 and c < 2:
                project(c + 1)
            ahead = enter(*units[j + 1])
        scores = jnp.concatenate([scores[:CUT], jnp.where(tail_ok, scores[CUT:], -1e30)], axis=0)
        expon = jnp.exp(scores - jnp.max(scores, axis=0, keepdims=True))
        probs = (expon * (1.0 / jnp.sum(expon, axis=0, keepdims=True))).astype(BF16)
        probs_ref[i, c] = probs
        heads_ref[i, :, c * 128 : c * 128 + 128] = own_heads(dot(v_turned, probs)).astype(BF16)


def mlp_kernel(
    places, places2, rows, blocks, fs, p0, p1, p2, p3, r0, r1, r2, r3, x_ref, og_ref, h_ref, gain_ref,
    y_ref, mg_ref, hg_ref, keep1, send1, keep2, send2,
    scr, w_out, w_back, w_fc1, w_fc1_turned, fc2_ref, w_fc2_turned, n2_all, pg_all, hid_all, og_all, ml_all, h_all, y_all,
):
    step = pl.program_id(0)

    @pl.when(step == 0)
    def _():
        unpack(places2, rows, (p0, p1, p2, p3), scr)
        unpack(places, rows, (r0, r1, r2, r3), scr, 256 + fs)
        last = jnp.concatenate([scr[0, :, 128:192], scr[1, :, 128:192]], axis=1)
        h_all[:, D:] = jnp.zeros((h_all.shape[0], WIDE - D), BF16)
        for b, value in enumerate((scr[0, :, 0:128], scr[1, :, 0:128], last)):
            value = value.astype(BF16)
            w_back[:, b * 128 : b * 128 + 128] = value
            w_out[b * 128 : b * 128 + 128, :] = value.T
        for t in range(2):
            at = slice(t * fs, t * fs + fs)
            value = scr[t, :, 256 : 256 + fs].astype(BF16)
            w_fc1[:, at] = value
            w_fc1_turned[at, :] = value.T
            value = scr[t, :, 256 + fs :].astype(BF16)
            fc2_ref[:, at] = value
            w_fc2_turned[at, :] = value.T

    @pl.when(step < blocks)
    def _():
        size = PER * PAD
        at = pl.ds(pl.multiple_of(step * size, size), size)
        gain = gain_ref[1:2, :]
        h = tall(h_ref)
        og = tall(og_ref)
        h_all[at, :D] = h
        og_all[at, :] = og
        middle = tall(x_ref).astype(F32) + dot(h, w_out[...])
        xhat, rstd = normalize(middle)
        n2 = (xhat * gain).astype(BF16)
        n2_all[at, :] = n2
        width = 256
        back = None
        count = 2 * fs // width
        ahead = dot(n2, w_fc1[:, :width]), dot(og, fc2_ref[:, :width])
        for c in range(count):
            cols = slice(c * width, c * width + width)
            u, dh = ahead
            if c + 1 < count:
                after = slice(c * width + width, c * width + 2 * width)
                ahead = dot(n2, w_fc1[:, after]), dot(og, fc2_ref[:, after])
            square = u * u
            bent = jnp.tanh(u * (GELU_C + (GELU_C * 0.044715) * square))
            plus = 0.5 + 0.5 * bent
            full = u * plus
            hid = full.astype(BF16)
            hid_all[at, cols] = hid
            slope = plus + full * (1.0 - plus) * ((2.0 * GELU_C) + (GELU_C * 0.26829) * square)
            pg = (dh * slope).astype(BF16)
            pg_all[at, cols] = pg
            part = dot(pg, w_fc1_turned[cols, :])
            back = part if back is None else back + part
            middle += dot(hid, w_fc2_turned[cols, :])
        store_rows(y_all, middle, step, blocks)
        mg = og.astype(F32) + norm_back(back, xhat, rstd, gain)
        mg_ref[...] = mg.reshape(PER, PAD, D)
        ml = mg.astype(BF16)
        ml_all[at, :] = ml
        hg_ref[...] = dot(ml, w_back[...]).astype(BF16).reshape(PER, PAD, D)

    @pl.when(step == blocks)
    def _():
        row_sum = jnp.zeros((D, 1), F32)
        for base, left, right in ((256, n2_all, pg_all), (256 + fs, og_all, hid_all)):
            turned = left[...].T
            for c in range(2 * fs // WIDE):
                cols = slice(c * WIDE, c * WIDE + WIDE)
                grad = dot(turned, right[:, cols])
                for piece in range(2):
                    t, at = divmod(c * WIDE + piece * 256, fs)
                    scr[t, :, base + at : base + at + 256] = grad[:, piece * 256 : piece * 256 + 256]
                if right is pg_all:
                    row_sum += jnp.sum(grad * w_fc1[:, cols].astype(F32), axis=1, keepdims=True)
        grad = dot(ml_all[...].T, h_all[...])
        scr[0, :, 0:128] = grad[:, 0:128]
        scr[1, :, 0:128] = grad[:, 128:256]
        gain = jnp.broadcast_to(row_sum, (D, HD))
        scr[0, :, 128:256] = jnp.concatenate([grad[:, 256 : 256 + HD], gain], axis=1)
        scr[1, :, 128:256] = jnp.concatenate([grad[:, 256 + HD : 384], gain], axis=1)
        repack(places, rows, scr, (keep1, send1))
        repack(places2, rows, scr, (keep2, send2), 256 + fs)
        y_ref[...] = y_all[...].astype(BF16)


def attend_back(qkv_ref, probs_ref, hg_ref, grad_ref, grad_all, at):
    low = low_lanes()
    units = [(i, c) for i in range(PER) for c in range(3)]

    def enter(i, c):
        do = both_heads(hg_ref[i, :, c * 128 : c * 128 + 128], low)
        return dot(qkv_ref[i, :, lanes(2, c)], do, NT), do

    ahead = enter(*units[0])
    for j, (i, c) in enumerate(units):
        dp, do = ahead
        if j + 1 < len(units):
            ahead = enter(*units[j + 1])
        low_probs = probs_ref[i, c]
        probs = low_probs.astype(F32)
        weighted = probs * dp
        ds = (weighted - probs * jnp.sum(weighted, axis=0, keepdims=True)).astype(BF16)
        q, k = qkv_ref[i, :, lanes(0, c)], qkv_ref[i, :, lanes(1, c)]
        dv = dot(low_probs, do)
        dk = dot(ds, both_heads(q, low))
        dq = own_heads(dot(k.T, ds)) * (HD**-0.5)
        for kind, value in enumerate((dq, dk, dv)):
            value = value.astype(BF16)
            grad_ref[i, :, lanes(kind, c)] = value
            if grad_all is not None:
                grad_all[pl.ds(pl.multiple_of(at + i * PAD, PAD), PAD), lanes(kind, c)] = value


def attend_back_kernel(qkv_ref, probs_ref, hg_ref, grad_ref):
    attend_back(qkv_ref, probs_ref, hg_ref, grad_ref, None, 0)


def attend_last_kernel(
    places, rows, blocks, qkv_ref, probs_ref, hg_ref, n1_ref, w_ref, *refs
):
    *earlier, grad_ref, keep, send, scr, grad_all = refs
    step = pl.program_id(0)
    early = sum(ref.shape[0] for ref in earlier) * PAD

    @pl.when(step == 0)
    def _():
        at = 0
        for ref in earlier:
            size = ref.shape[0] * PAD
            grad_all[at : at + size, :] = ref[...].reshape(size, 3 * D)
            at += size

    @pl.when(step < blocks)
    def _():
        attend_back(qkv_ref, probs_ref, hg_ref, grad_ref, grad_all, early + step * PER * PAD)

    @pl.when(step == blocks)
    def _():
        turned = n1_ref[...].reshape(-1, D).T
        row_sum = jnp.zeros((D, 1), F32)
        singles = [None] * 3
        for b in (8, 4, 0):
            some = range(b, min(b + 4, 9))
            span = slice(b * 128, some.stop * 128)
            grad = dot(turned, grad_all[:, span])
            row_sum += jnp.sum(grad * w_ref[:, span].astype(F32), axis=1, keepdims=True)
            for at in some:
                here = grad[:, (at - b) * 128 : (at - b) * 128 + 128]
                if at < 6:
                    scr[at // 3, :, at % 3 * 128 : at % 3 * 128 + 128] = here
                else:
                    singles[at - 6] = here
            if b == 4:
                for t in range(2):
                    own = [s[:, t * HD : t * HD + HD] for s in singles]
                    scr[t, :, 384:512] = jnp.concatenate(own[:2], axis=1)
                    scr[t, :, 512 : 512 + HD] = own[2]
        scr[:, :, 512 + HD : 640] = jnp.broadcast_to(row_sum[None], (2, D, HD))
        repack(places, rows, scr, (keep, send))


def store_rows(ref, value, step, steps):
    for s in range(steps):

        @pl.when(step == s)
        def _(s=s):
            for i in range(PER):
                at = (s * PER + i) * SEQ
                ref[at : at + SEQ, :] = value[i * PAD : i * PAD + SEQ]


def input_grad_kernel(cuts, *refs):
    *pieces, w_ref, x_ref, mg_ref, gain_ref, out_ref, w_turned, grad = refs
    step = pl.program_id(0)

    @pl.when(step == 0)
    def _():
        w_turned[:, :D] = w_ref[...].T
        w_turned[:, D:] = jnp.zeros((w_turned.shape[0], WIDE - D), BF16)

    at = 0
    for ref, count in zip(pieces, cuts, strict=True):

        @pl.when((step >= at) & (step < at + count))
        def _(ref=ref):
            grad[...] = tall(ref)

        at += count
    xhat, rstd = normalize(tall(x_ref).astype(F32))
    back = dot(grad[...], w_turned[...])[:, :D]
    dx = tall(mg_ref) + norm_back(back, xhat, rstd, gain_ref[0:1, :])
    store_rows(out_ref, dx, step, sum(cuts))


def finish_kernel(fs, mine_q, got_q, mine, got, gain1, gain2, ln1, qkv_grad, ln2, out_grad, fc1_grad, fc2_grad):
    total = mine_q[0].astype(F32) + got_q[0].astype(F32)
    for c in range(3):
        qkv_grad[c, :, 0:128] = total[:, c * 128 : c * 128 + 128]
        qkv_grad[c, :, 128:192] = total[:, 384 + c * HD : 448 + c * HD]
    ln1[...] = line(total[:, 576:577]) / gain1[...].astype(BF16).astype(F32)
    total = mine[0].astype(F32) + got[0].astype(F32)
    out_grad[...] = total[:, :192]
    fc1_grad[...] = total[:, 256 : 256 + fs]
    fc2_grad[...] = total[:, 256 + fs :]
    ln2[...] = line(total[:, 192:193]) / gain2[...].astype(BF16).astype(F32)


def whole(*shape):
    return pl.BlockSpec(shape, lambda *i: (0,) * len(shape))


def once(*shape):
    return pl.BlockSpec(shape, lambda *i: (0,) * len(shape), pipeline_mode=pl.Buffered(1))


def part(first, count, *shape):
    return pl.BlockSpec((PER,) + shape, lambda i: (first + jnp.minimum(i, count - 1),) + (0,) * len(shape))


def late(first, count, *shape):
    return pl.BlockSpec((PER,) + shape, lambda i: (jnp.clip(i - first, 0, count - 1),) + (0,) * len(shape))


def call(kernel, grid, ins, outs, scratch, args, mflops=0, kbytes=0, vmem=8):
    return pl.pallas_call(
        kernel,
        grid=(grid,) if grid else (),
        in_specs=ins,
        out_specs=[spec for spec, _ in outs],
        out_shape=[shape for _, shape in outs],
        scratch_shapes=scratch,
        compiler_params=pltpu.CompilerParams(vmem_limit_bytes=vmem * 1024 * 1024),
        cost_estimate=pl.CostEstimate(flops=mflops * 10**6, bytes_accessed=kbytes * 1000, transcendentals=0),
    )(*args)


def shape_of(*shape, dtype=BF16):
    return jax.ShapeDtypeStruct(shape, dtype)


def padded(v, images):
    return jnp.pad(v.reshape(images, SEQ, D), ((0, 0), (0, PAD - SEQ), (0, 0)))


def local(sizes, tokens, ln1_gain, qkv_weight, out_weight, ln2_gain, fc1_weight, fc2_weight, out_grad):
    return layer(sizes, tokens, ln1_gain, qkv_weight, out_weight, ln2_gain, fc1_weight, fc2_weight, out_grad)


def layer(sizes, tokens, ln1_gain, qkv_weight, out_weight, ln2_gain, fc1_weight, fc2_weight, out_grad):
    stages = stage_bits(sizes["wide"])
    stages2 = stages[:-3] + [stages[-2], stages[-3], stages[-1]]
    places, places2 = relative(stages), relative(stages2)
    n = len(places)
    rows = own_rows = qkv_weight.shape[0]
    images = tokens.shape[0] // SEQ
    blocks = images // PER
    fs = fc1_weight.shape[1]
    ff = 2 * fs
    rc = 256 + 2 * fs
    big = images * PAD
    gain1, gain2 = ln1_gain.reshape(1, rows), ln2_gain.reshape(1, rows)

    first, rest = call(
        pack_kernel,
        0,
        [whole(3, rows, 192), whole(1, rows), whole(1, rows), whole(rows, 192), whole(rows, fs), whole(rows, fs)],
        [(whole(1, rows, QC), shape_of(1, rows, QC)), (whole(1, rows, rc), shape_of(1, rows, rc))],
        [],
        (qkv_weight.transpose(1, 0, 2), gain1, gain2, out_weight.T, fc1_weight, fc2_weight.T),
        vmem=60,
    )
    first_all = gather(first, stages, sizes)
    for stage in stages[:-3]:
        rest = grow(rest, stage, sizes)
    rest1_all = gather(rest[:, :, : 256 + fs], stages2[-3:], sizes)
    rest2_all = gather(rest[:, :, 256 + fs :], stages[-3:], sizes)
    if rows % 8 != 0:
        n, rows = 16, 48
        first_all, rest1_all, rest2_all = (
            jnp.split(in_order(order, jnp.concatenate(v, axis=0)), 4)
            for order, v in ((places, first_all), (places2, rest1_all), (places, rest2_all))
        )

    x = padded(tokens, images)
    og = padded(out_grad, images)

    def row(*shape):
        return part(0, blocks, *shape)

    qkv, probs, heads, n1, w_qkv, gain = call(
        functools.partial(attend_kernel, places, rows),
        blocks,
        [once(n // 4, rows, QC)] * 4 + [row(PAD, D)],
        [
            (row(PAD, 3 * D), shape_of(images, PAD, 3 * D)),
            (row(3, PAD, WIDE), shape_of(images, 3, PAD, WIDE)),
            (row(PAD, D), shape_of(images, PAD, D)),
            (row(PAD, D), shape_of(images, PAD, D)),
            (whole(D, 3 * D), shape_of(D, 3 * D)),
            (whole(8, D), shape_of(8, D, dtype=F32)),
        ],
        [pltpu.VMEM((2, D, QC), F32)],
        (*first_all, x),
        8000,
        20000,
        24,
    )
    wide1, wide2 = 256 + fs, fs
    y, mg, hg, keep1, send1, keep2, send2 = call(
        functools.partial(mlp_kernel, places, places2, rows, blocks, fs),
        blocks + 1,
        [once(n // 4, rows, wide1)] * 4
        + [once(n // 4, rows, wide2)] * 4
        + [row(PAD, D), row(PAD, D), row(PAD, D), whole(8, D)],
        [
            (once(images * SEQ, D), shape_of(images * SEQ, D)),
            (row(PAD, D), shape_of(images, PAD, D, dtype=F32)),
            (row(PAD, D), shape_of(images, PAD, D)),
        ]
        + [(once(n // 2, rows, w), shape_of(n // 2, rows, w)) for w in (wide1, wide1, wide2, wide2)],
        [
            pltpu.VMEM((2, D, rc), F32),
            pltpu.VMEM((D, D), BF16),
            pltpu.VMEM((D, D), BF16),
            pltpu.VMEM((D, ff), BF16),
            pltpu.VMEM((ff, D), BF16),
            pltpu.VMEM((D, ff), BF16),
            pltpu.VMEM((ff, D), BF16),
            pltpu.VMEM((big, D), BF16),
            pltpu.VMEM((big, ff), BF16),
            pltpu.VMEM((big, ff), BF16),
            pltpu.VMEM((big, D), BF16),
            pltpu.VMEM((big, D), BF16),
            pltpu.VMEM((big, WIDE), BF16),
            pltpu.VMEM((images * SEQ, D), F32),
        ],
        (*rest1_all, *rest2_all, x, og, heads, gain),
        16000,
        30000,
        44,
    )
    if rows != own_rows:
        keep1, send1 = jnp.split(out_of_order(places, jnp.concatenate([keep1, send1], axis=0), own_rows), 2)
        keep2, send2 = jnp.split(out_of_order(places2, jnp.concatenate([keep2, send2], axis=0), own_rows), 2)
    back, back2 = stages[::-1], stages2[::-1]
    total1 = add_got(keep1, swap(send1, back[0], sizes))
    total2 = add_got(keep2, swap(send2, back[0], sizes))
    for s in (1, 2):
        total1 = reduce_stage(total1, back[s], sizes)
        total2 = reduce_stage(total2, back2[s], sizes)
    total = jnp.concatenate([total1, total2], axis=2)
    for stage in back[3:-1]:
        total = reduce_stage(total, stage, sizes)
    got = swap(total[1:], back[-1], sizes)

    cuts = (blocks // 2, blocks - blocks // 2)
    pieces = []
    at = 0
    for count in cuts[:-1]:
        pieces += call(
            attend_back_kernel,
            count,
            [part(at, count, *s) for s in ((PAD, 3 * D), (3, PAD, WIDE), (PAD, D))],
            [(part(0, count, PAD, 3 * D), shape_of(count * PER, PAD, 3 * D))],
            [],
            (qkv, probs, hg),
            1800 * count,
            4000 * count,
            20,
        )
        at += count
    left = cuts[-1]
    last, keep_q, send_q = call(
        functools.partial(attend_last_kernel, places, rows, left),
        left + 1,
        [part(at, left, *s) for s in ((PAD, 3 * D), (3, PAD, WIDE), (PAD, D))]
        + [once(images, PAD, D), once(D, 3 * D)]
        + [once(count * PER, PAD, 3 * D) for count in cuts[:-1]],
        [(part(0, left, PAD, 3 * D), shape_of(left * PER, PAD, 3 * D))]
        + [(whole(n // 2, rows, QC), shape_of(n // 2, rows, QC))] * 2,
        [pltpu.VMEM((2, D, QC), F32), pltpu.VMEM((big, 3 * D), BF16)],
        (qkv, probs, hg, n1, w_qkv, *pieces),
        3500,
        8000,
        32,
    )
    pieces.append(last)
    starts = [sum(cuts[:c]) for c in range(len(cuts))]
    (dx,) = call(
        functools.partial(input_grad_kernel, cuts),
        blocks,
        [late(at, count, PAD, 3 * D) for at, count in zip(starts, cuts, strict=True)]
        + [whole(D, 3 * D), row(PAD, D), row(PAD, D), whole(8, D)],
        [(once(images * SEQ, D), shape_of(images * SEQ, D, dtype=F32))],
        [pltpu.VMEM((3 * D, WIDE), BF16), pltpu.VMEM((PER * PAD, 3 * D), BF16)],
        (*pieces, w_qkv, x, mg, gain),
        2000,
        10000,
        24,
    )
    if rows != own_rows:
        keep_q, send_q = jnp.split(out_of_order(places, jnp.concatenate([keep_q, send_q], axis=0), own_rows), 2)
    total_q = add_got(keep_q, swap(send_q, back[0], sizes))
    for stage in back[1:-1]:
        total_q = reduce_stage(total_q, stage, sizes)
    got_q = swap(total_q[1:], back[-1], sizes)
    ln1_grad, qkv_grad, ln2_grad, out_wgrad, fc1_grad, fc2_grad = call(
        functools.partial(finish_kernel, fs),
        0,
        [whole(2, own_rows, QC), whole(1, own_rows, QC), whole(2, own_rows, rc), whole(1, own_rows, rc)]
        + [whole(1, own_rows)] * 2,
        [
            (whole(*shape), shape_of(*shape, dtype=F32))
            for shape in (
                (1, own_rows),
                (3, own_rows, 192),
                (1, own_rows),
                (own_rows, 192),
                (own_rows, fs),
                (own_rows, fs),
            )
        ],
        [],
        (total_q, got_q, total, got, gain1, gain2),
    )
    return (
        y,
        dx,
        ln1_grad.reshape(own_rows),
        qkv_grad.transpose(1, 0, 2),
        out_wgrad.T,
        ln2_grad.reshape(own_rows),
        fc1_grad,
        fc2_grad.T,
    )


def solution(mesh):
    rows = P(("wide", "tensor"), None)
    weights = (
        P("wide"),
        P("wide", None, "tensor"),
        P("tensor", "wide"),
        P("wide"),
        P("wide", "tensor"),
        P("tensor", "wide"),
    )
    return jax.shard_map(
        functools.partial(local, dict(mesh.shape)),
        mesh=mesh,
        in_specs=(rows, *weights, rows),
        out_specs=(rows, rows, *weights),
        check_vma=False,
    )
```

```python
import functools

import jax
import jax.numpy as jnp
from jax import lax
from jax.experimental import pallas as pl
from jax.experimental.pallas import tpu as pltpu
from jax.sharding import PartitionSpec as P

HD = 64
SEQ = 197
PAD = 208
PER = 2
CUT = 192
WIDE = 512
LANES = 256
D = 384
QC = 640
F32 = jnp.float32
BF16 = jnp.bfloat16
NT = (((1,), (1,)), ((), ()))
GELU_C = 0.7978845608028654


def dot(a, b, dims=(((1,), (0,)), ((), ()))):
    return lax.dot_general(a, b, dims, preferred_element_type=F32)


def stage_bits(wide):
    bits = [("wide", 1 << k) for k in range(1, wide.bit_length() - 1)]
    bits = bits[:0:-1] + bits[:1]
    return bits + [("tensor", 1), ("wide", 1)]


def relative(stages):
    places = [(0, 0)]
    for axis, bit in stages:
        places = places + [(w ^ bit, t) if axis == "wide" else (w, t ^ bit) for w, t in places]
    return places


def swap(value, stage, sizes):
    axis, bit = stage
    return lax.ppermute(value, axis, [(i, i ^ bit) for i in range(sizes[axis])])


def gather(held, stages, sizes):
    for stage in stages[:-2]:
        held = grow(held, stage, sizes)
    got = swap(held, stages[-2], sizes)
    return [held, got, swap(held, stages[-1], sizes), swap(got, stages[-1], sizes)]


def grow(held, stage, sizes):
    got = swap(held, stage, sizes)
    return jnp.concatenate([held, got], axis=0)


def reduce_stage(total, stage, sizes):
    half = total.shape[0] // 2
    return add_got(total[:half], swap(total[half:], stage, sizes))


def add_got(keep, got):
    return (keep.astype(F32) + got.astype(F32)).astype(BF16)


def in_order(places, held):
    me_w, me_t = lax.axis_index("wide"), lax.axis_index("tensor")
    at = {place: p for p, place in enumerate(places)}
    wide = len(places) // 2
    table = jnp.array([[at[w, t] for w in range(wide)] for t in range(2)], jnp.int32)
    order = table[me_t ^ jnp.arange(2)[:, None], me_w ^ jnp.arange(wide)[None, :]]
    return held[order.reshape(-1)].reshape(16, 48, held.shape[2])


def out_of_order(places, blocks, rows):
    me_w, me_t = lax.axis_index("wide"), lax.axis_index("tensor")
    wide = len(places) // 2
    order = jnp.array([w for w, _ in places], jnp.int32) ^ me_w
    order += wide * (jnp.array([t for _, t in places], jnp.int32) ^ me_t)
    return blocks.reshape(len(places), rows, blocks.shape[2])[order]


def rows_of(places, rows):
    if rows == 48:
        me_w, me_t = 0, 0
        places = [(w, t) for t in range(2) for w in range(8)]
    else:
        me_w, me_t = lax.axis_index("wide"), lax.axis_index("tensor")
    for p, (w, t) in enumerate(places):
        yield p, me_t ^ t, pl.ds(pl.multiple_of((me_w ^ w) * rows, 8), rows)


def unpack(places, rows, pieces, scr, at=0):
    size = len(pieces[0])
    width = pieces[0].shape[-1]
    for p, t, where in rows_of(places, rows):
        scr[t, where, at : at + width] = pieces[p // size][p % size].astype(F32)


def repack(places, rows, scr, pieces, at=0):
    size = len(pieces[0])
    width = pieces[0].shape[-1]
    for p, t, where in rows_of(places, rows):
        pieces[p // size][p % size] = scr[t, where, at : at + width].astype(BF16)


def normalize(v):
    center = v - jnp.mean(v, axis=-1, keepdims=True)
    rstd = lax.rsqrt(jnp.mean(center * center, axis=-1, keepdims=True) + 1e-06)
    return center * rstd, rstd


def norm_back(grad, xhat, rstd, gain):
    g = grad * gain
    return rstd * (
        g
        - jnp.mean(g, axis=-1, keepdims=True)
        - xhat * jnp.mean(g * xhat, axis=-1, keepdims=True)
    )


def low_lanes():
    return lax.broadcasted_iota(jnp.int32, (PAD, 128), 1) < HD


def both_heads(value, low):
    zero = jnp.zeros_like(value)
    gap = jnp.zeros((LANES - PAD, 128), value.dtype)
    return jnp.concatenate([jnp.where(low, value, zero), gap, jnp.where(low, zero, value), gap], axis=0)


def own_heads(value):
    own = jnp.concatenate([value[:HD, :LANES], value[HD:, LANES:]], axis=0)
    return own.T[:PAD]


def lanes(kind, c):
    return slice((3 * c + kind) * 128, (3 * c + kind) * 128 + 128)


def tall(ref):
    return ref[...].reshape(PER * PAD, ref.shape[-1])


def column(row):
    n = row.shape[1]
    own = lax.broadcasted_iota(jnp.int32, (n, n), 0) == lax.broadcasted_iota(jnp.int32, (n, n), 1)
    return jnp.sum(jnp.where(own, jnp.broadcast_to(row, (n, n)), 0.0), axis=1, keepdims=True)


def line(col):
    n = col.shape[0]
    own = lax.broadcasted_iota(jnp.int32, (n, n), 0) == lax.broadcasted_iota(jnp.int32, (n, n), 1)
    return jnp.sum(jnp.where(own, jnp.broadcast_to(col, (n, n)), 0.0), axis=0, keepdims=True)


def pack_kernel(qkv, gain1, gain2, out, fc1, fc2, first, rest):
    rows = out.shape[0]
    fs = fc1.shape[1]
    lane = lax.broadcasted_iota(jnp.int32, (rows, HD), 1)
    gains = jnp.where(lane == 0, column(gain1[...]), jnp.where(lane == 1, column(gain2[...]), 0.0))
    for c in range(3):
        first[0, :, c * 128 : c * 128 + 128] = qkv[c, :, 0:128]
    single = [qkv[c, :, 128:192].astype(F32) for c in range(3)]
    first[0, :, 384:512] = jnp.concatenate(single[:2], axis=1).astype(BF16)
    first[0, :, 512:640] = jnp.concatenate([single[2], gains], axis=1).astype(BF16)
    rest[0, :, 0:128] = out[:, 0:128]
    pad = jnp.zeros((rows, HD), F32)
    rest[0, :, 128:256] = jnp.concatenate([out[:, 128:192].astype(F32), pad], axis=1).astype(BF16)
    rest[0, :, 256 : 256 + fs] = fc1[...]
    rest[0, :, 256 + fs :] = fc2[...]


def attend_kernel(places, rows, p0, p1, p2, p3, x_ref, qkv_ref, probs_ref, heads_ref, n1_ref, w_ref, gain_ref, scr):
    @pl.when(pl.program_id(0) == 0)
    def _():
        unpack(places, rows, (p0, p1, p2, p3), scr)
        for t in range(2):
            w_ref[:, t * D : t * D + D] = scr[t, :, 0:D].astype(BF16)
        for kind in range(3):
            one = slice(D + kind * HD, D + kind * HD + HD)
            last = jnp.concatenate([scr[0, :, one], scr[1, :, one]], axis=1)
            w_ref[:, lanes(kind, 2)] = last.astype(BF16)
        turned = scr[0, :, 512:640].T
        gain_ref[...] = turned[HD : HD + 8, :]

    xhat, _ = normalize(tall(x_ref).astype(F32))
    n1 = (xhat * gain_ref[0:1, :]).astype(BF16)
    n1_ref[...] = n1.reshape(PER, PAD, D)
    low = low_lanes()
    tail_ok = lax.broadcasted_iota(jnp.int32, (PAD - CUT, WIDE), 0) < SEQ - CUT

    def project(c):
        at = slice(c * WIDE, min(c * WIDE + WIDE, 3 * D))
        value = dot(n1, w_ref[:, at])
        for piece in range((at.stop - at.start) // 128):
            here = value[:, piece * 128 : piece * 128 + 128]
            if (c * 4 + piece) % 3 == 0:
                here = here * (HD**-0.5)
            span = slice(at.start + piece * 128, at.start + piece * 128 + 128)
            qkv_ref[:, :, span] = here.astype(BF16).reshape(PER, PAD, 128)

    def enter(i, c):
        q, k, v = (qkv_ref[i, :, lanes(kind, c)] for kind in range(3))
        return dot(k, both_heads(q, low), NT), v.T

    units = [(i, c) for c in range(3) for i in range(PER)]
    project(0)
    ahead = enter(*units[0])
    for j, (i, c) in enumerate(units):
        scores, v_turned = ahead
        if j + 1 < len(units):
            if i == 0 and c < 2:
                project(c + 1)
            ahead = enter(*units[j + 1])
        scores = jnp.concatenate([scores[:CUT], jnp.where(tail_ok, scores[CUT:], -1e30)], axis=0)
        expon = jnp.exp(scores - jnp.max(scores, axis=0, keepdims=True))
        probs = (expon * (1.0 / jnp.sum(expon, axis=0, keepdims=True))).astype(BF16)
        probs_ref[i, c] = probs
        heads_ref[i, :, c * 128 : c * 128 + 128] = own_heads(dot(v_turned, probs)).astype(BF16)


def mlp_kernel(
    places, places2, rows, blocks, fs, p0, p1, p2, p3, r0, r1, r2, r3, x_ref, og_ref, h_ref, gain_ref,
    y_ref, mg_ref, hg_ref, keep1, send1, keep2, send2,
    scr, w_out, w_back, w_fc1, w_fc1_turned, fc2_ref, w_fc2_turned, n2_all, pg_all, hid_all, og_all, ml_all, h_all,
):
    step = pl.program_id(0)

    @pl.when(step == 0)
    def _():
        unpack(places2, rows, (p0, p1, p2, p3), scr)
        unpack(places, rows, (r0, r1, r2, r3), scr, 256 + fs)
        last = jnp.concatenate([scr[0, :, 128:192], scr[1, :, 128:192]], axis=1)
        h_all[:, D:] = jnp.zeros((h_all.shape[0], WIDE - D), BF16)
        for b, value in enumerate((scr[0, :, 0:128], scr[1, :, 0:128], last)):
            value = value.astype(BF16)
            w_back[:, b * 128 : b * 128 + 128] = value
            w_out[b * 128 : b * 128 + 128, :] = value.T
        for t in range(2):
            at = slice(t * fs, t * fs + fs)
            value = scr[t, :, 256 : 256 + fs].astype(BF16)
            w_fc1[:, at] = value
            w_fc1_turned[at, :] = value.T
            value = scr[t, :, 256 + fs :].astype(BF16)
            fc2_ref[:, at] = value
            w_fc2_turned[at, :] = value.T

    @pl.when(step < blocks)
    def _():
        size = PER * PAD
        at = pl.ds(pl.multiple_of(step * size, size), size)
        gain = gain_ref[1:2, :]
        h = tall(h_ref)
        og = tall(og_ref)
        h_all[at, :D] = h
        og_all[at, :] = og
        middle = tall(x_ref).astype(F32) + dot(h, w_out[...])
        xhat, rstd = normalize(middle)
        n2 = (xhat * gain).astype(BF16)
        n2_all[at, :] = n2
        width = 256
        back = None
        count = 2 * fs // width
        ahead = dot(n2, w_fc1[:, :width]), dot(og, fc2_ref[:, :width])
        for c in range(count):
            cols = slice(c * width, c * width + width)
            u, dh = ahead
            if c + 1 < count:
                after = slice(c * width + width, c * width + 2 * width)
                ahead = dot(n2, w_fc1[:, after]), dot(og, fc2_ref[:, after])
            square = u * u
            bent = jnp.tanh(u * (GELU_C + (GELU_C * 0.044715) * square))
            plus = 0.5 + 0.5 * bent
            full = u * plus
            hid = full.astype(BF16)
            hid_all[at, cols] = hid
            slope = plus + full * (1.0 - plus) * ((2.0 * GELU_C) + (GELU_C * 0.26829) * square)
            pg = (dh * slope).astype(BF16)
            pg_all[at, cols] = pg
            part = dot(pg, w_fc1_turned[cols, :])
            back = part if back is None else back + part
            middle += dot(hid, w_fc2_turned[cols, :])
        store_rows(y_ref, middle.astype(BF16), step, blocks)
        mg = og.astype(F32) + norm_back(back, xhat, rstd, gain)
        ml = mg.astype(BF16)
        mg_ref[...] = ml.reshape(PER, PAD, D)
        ml_all[at, :] = ml
        hg_ref[...] = dot(ml, w_back[...]).astype(BF16).reshape(PER, PAD, D)

    @pl.when(step == blocks)
    def _():
        row_sum = jnp.zeros((D, 1), F32)
        for base, left, right in ((256, n2_all, pg_all), (256 + fs, og_all, hid_all)):
            turned = left[...].T
            for c in range(2 * fs // WIDE):
                cols = slice(c * WIDE, c * WIDE + WIDE)
                grad = dot(turned, right[:, cols])
                for piece in range(2):
                    t, at = divmod(c * WIDE + piece * 256, fs)
                    scr[t, :, base + at : base + at + 256] = grad[:, piece * 256 : piece * 256 + 256]
                if right is pg_all:
                    row_sum += jnp.sum(grad * w_fc1[:, cols].astype(F32), axis=1, keepdims=True)
        grad = dot(ml_all[...].T, h_all[...])
        scr[0, :, 0:128] = grad[:, 0:128]
        scr[1, :, 0:128] = grad[:, 128:256]
        gain = jnp.broadcast_to(row_sum, (D, HD))
        scr[0, :, 128:256] = jnp.concatenate([grad[:, 256 : 256 + HD], gain], axis=1)
        scr[1, :, 128:256] = jnp.concatenate([grad[:, 256 + HD : 384], gain], axis=1)
        repack(places, rows, scr, (keep1, send1))
        repack(places2, rows, scr, (keep2, send2), 256 + fs)


def attend_back(qkv_ref, probs_ref, hg_ref, grad_ref, grad_all, at):
    low = low_lanes()
    units = [(i, c) for i in range(PER) for c in range(3)]

    def enter(i, c):
        do = both_heads(hg_ref[i, :, c * 128 : c * 128 + 128], low)
        return dot(qkv_ref[i, :, lanes(2, c)], do, NT), do

    ahead = enter(*units[0])
    for j, (i, c) in enumerate(units):
        dp, do = ahead
        if j + 1 < len(units):
            ahead = enter(*units[j + 1])
        low_probs = probs_ref[i, c]
        probs = low_probs.astype(F32)
        weighted = probs * dp
        ds = (weighted - probs * jnp.sum(weighted, axis=0, keepdims=True)).astype(BF16)
        q, k = qkv_ref[i, :, lanes(0, c)], qkv_ref[i, :, lanes(1, c)]
        dv = dot(low_probs, do)
        dk = dot(ds, both_heads(q, low))
        dq = own_heads(dot(k.T, ds)) * (HD**-0.5)
        for kind, value in enumerate((dq, dk, dv)):
            value = value.astype(BF16)
            grad_ref[i, :, lanes(kind, c)] = value
            if grad_all is not None:
                grad_all[pl.ds(pl.multiple_of(at + i * PAD, PAD), PAD), lanes(kind, c)] = value


def attend_back_kernel(qkv_ref, probs_ref, hg_ref, grad_ref):
    attend_back(qkv_ref, probs_ref, hg_ref, grad_ref, None, 0)


def attend_last_kernel(
    places, rows, blocks, qkv_ref, probs_ref, hg_ref, n1_ref, w_ref, *refs
):
    *earlier, grad_ref, keep, send, scr, grad_all = refs
    step = pl.program_id(0)
    early = sum(ref.shape[0] for ref in earlier) * PAD

    @pl.when(step == 0)
    def _():
        at = 0
        for ref in earlier:
            size = ref.shape[0] * PAD
            grad_all[at : at + size, :] = ref[...].reshape(size, 3 * D)
            at += size

    @pl.when(step < blocks)
    def _():
        attend_back(qkv_ref, probs_ref, hg_ref, grad_ref, grad_all, early + step * PER * PAD)

    @pl.when(step == blocks)
    def _():
        turned = n1_ref[...].reshape(-1, D).T
        row_sum = jnp.zeros((D, 1), F32)
        singles = [None] * 3
        for b in (8, 4, 0):
            some = range(b, min(b + 4, 9))
            span = slice(b * 128, some.stop * 128)
            grad = dot(turned, grad_all[:, span])
            row_sum += jnp.sum(grad * w_ref[:, span].astype(F32), axis=1, keepdims=True)
            for at in some:
                here = grad[:, (at - b) * 128 : (at - b) * 128 + 128]
                if at < 6:
                    scr[at // 3, :, at % 3 * 128 : at % 3 * 128 + 128] = here
                else:
                    singles[at - 6] = here
            if b == 4:
                for t in range(2):
                    own = [s[:, t * HD : t * HD + HD] for s in singles]
                    scr[t, :, 384:512] = jnp.concatenate(own[:2], axis=1)
                    scr[t, :, 512 : 512 + HD] = own[2]
        scr[:, :, 512 + HD : 640] = jnp.broadcast_to(row_sum[None], (2, D, HD))
        repack(places, rows, scr, (keep, send))


def store_rows(ref, value, step, steps):
    for s in range(steps):

        @pl.when(step == s)
        def _(s=s):
            for i in range(PER):
                at = (s * PER + i) * SEQ
                ref[at : at + SEQ, :] = value[i * PAD : i * PAD + SEQ]


def input_grad_kernel(cuts, *refs):
    *pieces, w_ref, x_ref, mg_ref, gain_ref, out_ref, w_turned, grad = refs
    step = pl.program_id(0)

    @pl.when(step == 0)
    def _():
        w_turned[:, :D] = w_ref[...].T
        w_turned[:, D:] = jnp.zeros((w_turned.shape[0], WIDE - D), BF16)

    at = 0
    for ref, count in zip(pieces, cuts, strict=True):

        @pl.when((step >= at) & (step < at + count))
        def _(ref=ref):
            grad[...] = tall(ref)

        at += count
    xhat, rstd = normalize(tall(x_ref).astype(F32))
    back = dot(grad[...], w_turned[...])[:, :D]
    dx = tall(mg_ref).astype(F32) + norm_back(back, xhat, rstd, gain_ref[0:1, :])
    store_rows(out_ref, dx, step, sum(cuts))


def finish_kernel(fs, mine_q, got_q, mine, got, gain1, gain2, ln1, qkv_grad, ln2, out_grad, fc1_grad, fc2_grad):
    total = mine_q[0].astype(F32) + got_q[0].astype(F32)
    for c in range(3):
        qkv_grad[c, :, 0:128] = total[:, c * 128 : c * 128 + 128]
        qkv_grad[c, :, 128:192] = total[:, 384 + c * HD : 448 + c * HD]
    ln1[...] = line(total[:, 576:577]) / gain1[...].astype(BF16).astype(F32)
    total = mine[0].astype(F32) + got[0].astype(F32)
    out_grad[...] = total[:, :192]
    fc1_grad[...] = total[:, 256 : 256 + fs]
    fc2_grad[...] = total[:, 256 + fs :]
    ln2[...] = line(total[:, 192:193]) / gain2[...].astype(BF16).astype(F32)


def whole(*shape):
    return pl.BlockSpec(shape, lambda *i: (0,) * len(shape))


def once(*shape):
    return pl.BlockSpec(shape, lambda *i: (0,) * len(shape), pipeline_mode=pl.Buffered(1))


def part(first, count, *shape):
    return pl.BlockSpec((PER,) + shape, lambda i: (first + jnp.minimum(i, count - 1),) + (0,) * len(shape))


def late(first, count, *shape):
    return pl.BlockSpec((PER,) + shape, lambda i: (jnp.clip(i - first, 0, count - 1),) + (0,) * len(shape))


def call(kernel, grid, ins, outs, scratch, args, mflops=0, kbytes=0, vmem=8):
    return pl.pallas_call(
        kernel,
        grid=(grid,) if grid else (),
        in_specs=ins,
        out_specs=[spec for spec, _ in outs],
        out_shape=[shape for _, shape in outs],
        scratch_shapes=scratch,
        compiler_params=pltpu.CompilerParams(vmem_limit_bytes=vmem * 1024 * 1024),
        cost_estimate=pl.CostEstimate(flops=mflops * 10**6, bytes_accessed=kbytes * 1000, transcendentals=0),
    )(*args)


def shape_of(*shape, dtype=BF16):
    return jax.ShapeDtypeStruct(shape, dtype)


def padded(v, images):
    return jnp.pad(v.reshape(images, SEQ, D), ((0, 0), (0, PAD - SEQ), (0, 0)))


def local(sizes, tokens, ln1_gain, qkv_weight, out_weight, ln2_gain, fc1_weight, fc2_weight, out_grad):
    return layer(sizes, tokens, ln1_gain, qkv_weight, out_weight, ln2_gain, fc1_weight, fc2_weight, out_grad)


def layer(sizes, tokens, ln1_gain, qkv_weight, out_weight, ln2_gain, fc1_weight, fc2_weight, out_grad):
    stages = stage_bits(sizes["wide"])
    stages2 = stages[:-3] + [stages[-2], stages[-3], stages[-1]]
    places, places2 = relative(stages), relative(stages2)
    n = len(places)
    rows = own_rows = qkv_weight.shape[0]
    images = tokens.shape[0] // SEQ
    blocks = images // PER
    fs = fc1_weight.shape[1]
    ff = 2 * fs
    rc = 256 + 2 * fs
    big = images * PAD
    gain1, gain2 = ln1_gain.reshape(1, rows), ln2_gain.reshape(1, rows)

    first, rest = call(
        pack_kernel,
        0,
        [whole(3, rows, 192), whole(1, rows), whole(1, rows), whole(rows, 192), whole(rows, fs), whole(rows, fs)],
        [(whole(1, rows, QC), shape_of(1, rows, QC)), (whole(1, rows, rc), shape_of(1, rows, rc))],
        [],
        (qkv_weight.transpose(1, 0, 2), gain1, gain2, out_weight.T, fc1_weight, fc2_weight.T),
        vmem=60,
    )
    first_all = gather(first, stages, sizes)
    for stage in stages[:-3]:
        rest = grow(rest, stage, sizes)
    rest1_all = gather(rest[:, :, : 256 + fs], stages2[-3:], sizes)
    rest2_all = gather(rest[:, :, 256 + fs :], stages[-3:], sizes)
    if rows % 8 != 0:
        n, rows = 16, 48
        first_all, rest1_all, rest2_all = (
            jnp.split(in_order(order, jnp.concatenate(v, axis=0)), 4)
            for order, v in ((places, first_all), (places2, rest1_all), (places, rest2_all))
        )

    x = padded(tokens, images)
    og = padded(out_grad, images)

    def row(*shape):
        return part(0, blocks, *shape)

    qkv, probs, heads, n1, w_qkv, gain = call(
        functools.partial(attend_kernel, places, rows),
        blocks,
        [once(n // 4, rows, QC)] * 4 + [row(PAD, D)],
        [
            (row(PAD, 3 * D), shape_of(images, PAD, 3 * D)),
            (row(3, PAD, WIDE), shape_of(images, 3, PAD, WIDE)),
            (row(PAD, D), shape_of(images, PAD, D)),
            (row(PAD, D), shape_of(images, PAD, D)),
            (whole(D, 3 * D), shape_of(D, 3 * D)),
            (whole(8, D), shape_of(8, D, dtype=F32)),
        ],
        [pltpu.VMEM((2, D, QC), F32)],
        (*first_all, x),
        8000,
        20000,
        24,
    )
    wide1, wide2 = 256 + fs, fs
    y, mg, hg, keep1, send1, keep2, send2 = call(
        functools.partial(mlp_kernel, places, places2, rows, blocks, fs),
        blocks + 1,
        [once(n // 4, rows, wide1)] * 4
        + [once(n // 4, rows, wide2)] * 4
        + [row(PAD, D), row(PAD, D), row(PAD, D), whole(8, D)],
        [
            (once(images * SEQ, D), shape_of(images * SEQ, D)),
            (row(PAD, D), shape_of(images, PAD, D)),
            (row(PAD, D), shape_of(images, PAD, D)),
        ]
        + [(once(n // 2, rows, w), shape_of(n // 2, rows, w)) for w in (wide1, wide1, wide2, wide2)],
        [
            pltpu.VMEM((2, D, rc), F32),
            pltpu.VMEM((D, D), BF16),
            pltpu.VMEM((D, D), BF16),
            pltpu.VMEM((D, ff), BF16),
            pltpu.VMEM((ff, D), BF16),
            pltpu.VMEM((D, ff), BF16),
            pltpu.VMEM((ff, D), BF16),
            pltpu.VMEM((big, D), BF16),
            pltpu.VMEM((big, ff), BF16),
            pltpu.VMEM((big, ff), BF16),
            pltpu.VMEM((big, D), BF16),
            pltpu.VMEM((big, D), BF16),
            pltpu.VMEM((big, WIDE), BF16),
        ],
        (*rest1_all, *rest2_all, x, og, heads, gain),
        16000,
        30000,
        34,
    )
    if rows != own_rows:
        keep1, send1 = jnp.split(out_of_order(places, jnp.concatenate([keep1, send1], axis=0), own_rows), 2)
        keep2, send2 = jnp.split(out_of_order(places2, jnp.concatenate([keep2, send2], axis=0), own_rows), 2)
    back, back2 = stages[::-1], stages2[::-1]
    total1 = add_got(keep1, swap(send1, back[0], sizes))
    total2 = add_got(keep2, swap(send2, back[0], sizes))
    for s in (1, 2):
        total1 = reduce_stage(total1, back[s], sizes)
        total2 = reduce_stage(total2, back2[s], sizes)
    total = jnp.concatenate([total1, total2], axis=2)
    for stage in back[3:-1]:
        total = reduce_stage(total, stage, sizes)
    got = swap(total[1:], back[-1], sizes)

    cuts = (blocks // 2, blocks - blocks // 2)
    pieces = []
    at = 0
    for count in cuts[:-1]:
        pieces += call(
            attend_back_kernel,
            count,
            [part(at, count, *s) for s in ((PAD, 3 * D), (3, PAD, WIDE), (PAD, D))],
            [(part(0, count, PAD, 3 * D), shape_of(count * PER, PAD, 3 * D))],
            [],
            (qkv, probs, hg),
            1800 * count,
            4000 * count,
            20,
        )
        at += count
    left = cuts[-1]
    last, keep_q, send_q = call(
        functools.partial(attend_last_kernel, places, rows, left),
        left + 1,
        [part(at, left, *s) for s in ((PAD, 3 * D), (3, PAD, WIDE), (PAD, D))]
        + [once(images, PAD, D), once(D, 3 * D)]
        + [once(count * PER, PAD, 3 * D) for count in cuts[:-1]],
        [(part(0, left, PAD, 3 * D), shape_of(left * PER, PAD, 3 * D))]
        + [(whole(n // 2, rows, QC), shape_of(n // 2, rows, QC))] * 2,
        [pltpu.VMEM((2, D, QC), F32), pltpu.VMEM((big, 3 * D), BF16)],
        (qkv, probs, hg, n1, w_qkv, *pieces),
        3500,
        8000,
        32,
    )
    pieces.append(last)
    starts = [sum(cuts[:c]) for c in range(len(cuts))]
    (dx,) = call(
        functools.partial(input_grad_kernel, cuts),
        blocks,
        [late(at, count, PAD, 3 * D) for at, count in zip(starts, cuts, strict=True)]
        + [whole(D, 3 * D), row(PAD, D), row(PAD, D), whole(8, D)],
        [(once(images * SEQ, D), shape_of(images * SEQ, D, dtype=F32))],
        [pltpu.VMEM((3 * D, WIDE), BF16), pltpu.VMEM((PER * PAD, 3 * D), BF16)],
        (*pieces, w_qkv, x, mg, gain),
        2000,
        10000,
        24,
    )
    if rows != own_rows:
        keep_q, send_q = jnp.split(out_of_order(places, jnp.concatenate([keep_q, send_q], axis=0), own_rows), 2)
    total_q = add_got(keep_q, swap(send_q, back[0], sizes))
    for stage in back[1:-1]:
        total_q = reduce_stage(total_q, stage, sizes)
    got_q = swap(total_q[1:], back[-1], sizes)
    ln1_grad, qkv_grad, ln2_grad, out_wgrad, fc1_grad, fc2_grad = call(
        functools.partial(finish_kernel, fs),
        0,
        [whole(2, own_rows, QC), whole(1, own_rows, QC), whole(2, own_rows, rc), whole(1, own_rows, rc)]
        + [whole(1, own_rows)] * 2,
        [
            (whole(*shape), shape_of(*shape, dtype=F32))
            for shape in (
                (1, own_rows),
                (3, own_rows, 192),
                (1, own_rows),
                (own_rows, 192),
                (own_rows, fs),
                (own_rows, fs),
            )
        ],
        [],
        (total_q, got_q, total, got, gain1, gain2),
    )
    return (
        y,
        dx,
        ln1_grad.reshape(own_rows),
        qkv_grad.transpose(1, 0, 2),
        out_wgrad.T,
        ln2_grad.reshape(own_rows),
        fc1_grad,
        fc2_grad.T,
    )


def solution(mesh):
    rows = P(("wide", "tensor"), None)
    weights = (
        P("wide"),
        P("wide", None, "tensor"),
        P("tensor", "wide"),
        P("wide"),
        P("wide", "tensor"),
        P("tensor", "wide"),
    )
    return jax.shard_map(
        functools.partial(local, dict(mesh.shape)),
        mesh=mesh,
        in_specs=(rows, *weights, rows),
        out_specs=(rows, rows, *weights),
        check_vma=False,
    )
```

```python
import functools

import jax
import jax.numpy as jnp
from jax import lax
from jax.experimental import pallas as pl
from jax.experimental.pallas import tpu as pltpu
from jax.sharding import PartitionSpec as P

HD = 64
SEQ = 197
PAD = 208
PER = 2
CUT = 192
WIDE = 512
LANES = 256
D = 384
QC = 640
F32 = jnp.float32
BF16 = jnp.bfloat16
NT = (((1,), (1,)), ((), ()))
GELU_C = 0.7978845608028654


def dot(a, b, dims=(((1,), (0,)), ((), ()))):
    return lax.dot_general(a, b, dims, preferred_element_type=F32)


def stage_bits(wide):
    bits = [("wide", 1 << k) for k in range(1, wide.bit_length() - 1)]
    bits = bits[:0:-1] + bits[:1]
    return bits + [("tensor", 1), ("wide", 1)]


def relative(stages):
    places = [(0, 0)]
    for axis, bit in stages:
        places = places + [(w ^ bit, t) if axis == "wide" else (w, t ^ bit) for w, t in places]
    return places


def swap(value, stage, sizes):
    axis, bit = stage
    return lax.ppermute(value, axis, [(i, i ^ bit) for i in range(sizes[axis])])


def gather(held, stages, sizes):
    for stage in stages[:-2]:
        held = grow(held, stage, sizes)
    got = swap(held, stages[-2], sizes)
    return [held, got, swap(held, stages[-1], sizes), swap(got, stages[-1], sizes)]


def grow(held, stage, sizes):
    got = swap(held, stage, sizes)
    return jnp.concatenate([held, got], axis=0)


def reduce_stage(total, stage, sizes):
    half = total.shape[0] // 2
    return add_got(total[:half], swap(total[half:], stage, sizes))


def add_got(keep, got):
    return (keep.astype(F32) + got.astype(F32)).astype(BF16)


def in_order(places, held):
    me_w, me_t = lax.axis_index("wide"), lax.axis_index("tensor")
    at = {place: p for p, place in enumerate(places)}
    wide = len(places) // 2
    table = jnp.array([[at[w, t] for w in range(wide)] for t in range(2)], jnp.int32)
    order = table[me_t ^ jnp.arange(2)[:, None], me_w ^ jnp.arange(wide)[None, :]]
    return held[order.reshape(-1)].reshape(16, 48, held.shape[2])


def out_of_order(places, blocks, rows):
    me_w, me_t = lax.axis_index("wide"), lax.axis_index("tensor")
    wide = len(places) // 2
    order = jnp.array([w for w, _ in places], jnp.int32) ^ me_w
    order += wide * (jnp.array([t for _, t in places], jnp.int32) ^ me_t)
    return blocks.reshape(len(places), rows, blocks.shape[2])[order]


def rows_of(places, rows):
    if rows == 48:
        me_w, me_t = 0, 0
        places = [(w, t) for t in range(2) for w in range(8)]
    else:
        me_w, me_t = lax.axis_index("wide"), lax.axis_index("tensor")
    for p, (w, t) in enumerate(places):
        yield p, me_t ^ t, pl.ds(pl.multiple_of((me_w ^ w) * rows, 8), rows)


def unpack(places, rows, pieces, scr, at=0):
    size = len(pieces[0])
    width = pieces[0].shape[-1]
    for p, t, where in rows_of(places, rows):
        scr[t, where, at : at + width] = pieces[p // size][p % size].astype(F32)


def repack(places, rows, scr, pieces, at=0):
    size = len(pieces[0])
    width = pieces[0].shape[-1]
    for p, t, where in rows_of(places, rows):
        pieces[p // size][p % size] = scr[t, where, at : at + width].astype(BF16)


def normalize(v):
    center = v - jnp.mean(v, axis=-1, keepdims=True)
    rstd = lax.rsqrt(jnp.mean(center * center, axis=-1, keepdims=True) + 1e-06)
    return center * rstd, rstd


def norm_back(grad, xhat, rstd, gain):
    g = grad * gain
    return rstd * (
        g
        - jnp.mean(g, axis=-1, keepdims=True)
        - xhat * jnp.mean(g * xhat, axis=-1, keepdims=True)
    )


def low_lanes():
    return lax.broadcasted_iota(jnp.int32, (PAD, 128), 1) < HD


def both_heads(value, low):
    zero = jnp.zeros_like(value)
    gap = jnp.zeros((LANES - PAD, 128), value.dtype)
    return jnp.concatenate([jnp.where(low, value, zero), gap, jnp.where(low, zero, value), gap], axis=0)


def own_heads(value):
    own = jnp.concatenate([value[:HD, :LANES], value[HD:, LANES:]], axis=0)
    return own.T[:PAD]


def lanes(kind, c):
    return slice((3 * c + kind) * 128, (3 * c + kind) * 128 + 128)


def tall(ref):
    return ref[...].reshape(PER * PAD, ref.shape[-1])


def column(row):
    n = row.shape[1]
    own = lax.broadcasted_iota(jnp.int32, (n, n), 0) == lax.broadcasted_iota(jnp.int32, (n, n), 1)
    return jnp.sum(jnp.where(own, jnp.broadcast_to(row, (n, n)), 0.0), axis=1, keepdims=True)


def line(col):
    n = col.shape[0]
    own = lax.broadcasted_iota(jnp.int32, (n, n), 0) == lax.broadcasted_iota(jnp.int32, (n, n), 1)
    return jnp.sum(jnp.where(own, jnp.broadcast_to(col, (n, n)), 0.0), axis=0, keepdims=True)


def pack_kernel(qkv, gain1, gain2, out, fc1, fc2, first, rest, rest2):
    rows = out.shape[0]
    fs = fc1.shape[1]
    lane = lax.broadcasted_iota(jnp.int32, (rows, HD), 1)
    gains = jnp.where(lane == 0, column(gain1[...]), jnp.where(lane == 1, column(gain2[...]), 0.0))
    for c in range(3):
        first[0, :, c * 128 : c * 128 + 128] = qkv[c, :, 0:128]
    single = [qkv[c, :, 128:192].astype(F32) for c in range(3)]
    first[0, :, 384:512] = jnp.concatenate(single[:2], axis=1).astype(BF16)
    first[0, :, 512:640] = jnp.concatenate([single[2], gains], axis=1).astype(BF16)
    rest[0, :, 0:128] = out[:, 0:128]
    pad = jnp.zeros((rows, HD), F32)
    rest[0, :, 128:256] = jnp.concatenate([out[:, 128:192].astype(F32), pad], axis=1).astype(BF16)
    rest[0, :, 256 : 256 + fs] = fc1[...]
    rest2[0] = fc2[...]


def pad_kernel(tokens, out_grad, x_ref, og_ref):
    tail = jnp.zeros((PAD - SEQ, D), F32)
    for source, target in ((tokens, x_ref), (out_grad, og_ref)):
        for i in range(target.shape[0]):
            own = source[i * SEQ : i * SEQ + SEQ, :].astype(F32)
            target[i] = jnp.concatenate([own, tail], axis=0).astype(BF16)


def attend_kernel(places, rows, p0, p1, p2, p3, x_ref, qkv_ref, probs_ref, heads_ref, n1_ref, w_ref, gain_ref, scr):
    @pl.when(pl.program_id(0) == 0)
    def _():
        unpack(places, rows, (p0, p1, p2, p3), scr)
        for t in range(2):
            w_ref[:, t * D : t * D + D] = scr[t, :, 0:D].astype(BF16)
        for kind in range(3):
            one = slice(D + kind * HD, D + kind * HD + HD)
            last = jnp.concatenate([scr[0, :, one], scr[1, :, one]], axis=1)
            w_ref[:, lanes(kind, 2)] = last.astype(BF16)
        turned = scr[0, :, 512:640].T
        gain_ref[...] = turned[HD : HD + 8, :]

    xhat, _ = normalize(tall(x_ref).astype(F32))
    n1 = (xhat * gain_ref[0:1, :]).astype(BF16)
    n1_ref[...] = n1.reshape(PER, PAD, D)
    low = low_lanes()
    tail_ok = lax.broadcasted_iota(jnp.int32, (PAD - CUT, WIDE), 0) < SEQ - CUT

    def project(c):
        at = slice(c * WIDE, min(c * WIDE + WIDE, 3 * D))
        value = dot(n1, w_ref[:, at])
        for piece in range((at.stop - at.start) // 128):
            here = value[:, piece * 128 : piece * 128 + 128]
            if (c * 4 + piece) % 3 == 0:
                here = here * (HD**-0.5)
            span = slice(at.start + piece * 128, at.start + piece * 128 + 128)
            qkv_ref[:, :, span] = here.astype(BF16).reshape(PER, PAD, 128)

    def enter(i, c):
        q, k, v = (qkv_ref[i, :, lanes(kind, c)] for kind in range(3))
        return dot(k, both_heads(q, low), NT), v.T

    units = [(i, c) for c in range(3) for i in range(PER)]
    project(0)
    ahead = enter(*units[0])
    for j, (i, c) in enumerate(units):
        scores, v_turned = ahead
        if j + 1 < len(units):
            if i == 0 and c < 2:
                project(c + 1)
            ahead = enter(*units[j + 1])
        scores = jnp.concatenate([scores[:CUT], jnp.where(tail_ok, scores[CUT:], -1e30)], axis=0)
        expon = jnp.exp(scores - jnp.max(scores, axis=0, keepdims=True))
        probs = (expon * (1.0 / jnp.sum(expon, axis=0, keepdims=True))).astype(BF16)
        probs_ref[i, c] = probs
        heads_ref[i, :, c * 128 : c * 128 + 128] = own_heads(dot(v_turned, probs)).astype(BF16)


def mlp_kernel(
    places, places2, rows, blocks, fs, p0, p1, p2, p3, r0, r1, r2, r3, x_ref, og_ref, h_ref, gain_ref,
    y_ref, mg_ref, hg_ref, keep1, send1, keep2, send2,
    scr, w_back, w_fc1, fc2_ref, n2_all, pg_all, hid_all, og_all, ml_all, h_all,
):
    step = pl.program_id(0)

    @pl.when(step == 0)
    def _():
        unpack(places2, rows, (p0, p1, p2, p3), scr)
        unpack(places, rows, (r0, r1, r2, r3), scr, 256 + fs)
        last = jnp.concatenate([scr[0, :, 128:192], scr[1, :, 128:192]], axis=1)
        h_all[:, D:] = jnp.zeros((h_all.shape[0], WIDE - D), BF16)
        for b, value in enumerate((scr[0, :, 0:128], scr[1, :, 0:128], last)):
            value = value.astype(BF16)
            w_back[:, b * 128 : b * 128 + 128] = value
        for t in range(2):
            at = slice(t * fs, t * fs + fs)
            value = scr[t, :, 256 : 256 + fs].astype(BF16)
            w_fc1[:, at] = value
            value = scr[t, :, 256 + fs :].astype(BF16)
            fc2_ref[:, at] = value

    @pl.when(step < blocks)
    def _():
        size = PER * PAD
        at = pl.ds(pl.multiple_of(step * size, size), size)
        gain = gain_ref[1:2, :]
        h = tall(h_ref)
        og = tall(og_ref)
        h_all[at, :D] = h
        og_all[at, :] = og
        middle = tall(x_ref).astype(F32) + dot(h, w_back[...], NT)
        xhat, rstd = normalize(middle)
        n2 = (xhat * gain).astype(BF16)
        n2_all[at, :] = n2
        width = 256
        back = None
        count = 2 * fs // width
        ahead = dot(n2, w_fc1[:, :width]), dot(og, fc2_ref[:, :width])
        for c in range(count):
            cols = slice(c * width, c * width + width)
            u, dh = ahead
            if c + 1 < count:
                after = slice(c * width + width, c * width + 2 * width)
                ahead = dot(n2, w_fc1[:, after]), dot(og, fc2_ref[:, after])
            square = u * u
            bent = jnp.tanh(u * (GELU_C + (GELU_C * 0.044715) * square))
            plus = 0.5 + 0.5 * bent
            full = u * plus
            hid = full.astype(BF16)
            hid_all[at, cols] = hid
            slope = plus + full * (1.0 - plus) * ((2.0 * GELU_C) + (GELU_C * 0.26829) * square)
            pg = (dh * slope).astype(BF16)
            pg_all[at, cols] = pg
            part = dot(pg, w_fc1[:, cols], NT)
            back = part if back is None else back + part
            middle += dot(hid, fc2_ref[:, cols], NT)
        store_rows(y_ref, middle.astype(BF16), step, blocks)
        mg = og.astype(F32) + norm_back(back, xhat, rstd, gain)
        ml = mg.astype(BF16)
        mg_ref[...] = ml.reshape(PER, PAD, D)
        ml_all[at, :] = ml
        hg_ref[...] = dot(ml, w_back[...]).astype(BF16).reshape(PER, PAD, D)

    @pl.when(step == blocks)
    def _():
        row_sum = jnp.zeros((D, 1), F32)
        for base, left, right in ((256, n2_all, pg_all), (256 + fs, og_all, hid_all)):
            turned = left[...].T
            for c in range(2 * fs // WIDE):
                cols = slice(c * WIDE, c * WIDE + WIDE)
                grad = dot(turned, right[:, cols])
                for piece in range(2):
                    t, at = divmod(c * WIDE + piece * 256, fs)
                    scr[t, :, base + at : base + at + 256] = grad[:, piece * 256 : piece * 256 + 256]
                if right is pg_all:
                    row_sum += jnp.sum(grad * w_fc1[:, cols].astype(F32), axis=1, keepdims=True)
        grad = dot(ml_all[...].T, h_all[...])
        scr[0, :, 0:128] = grad[:, 0:128]
        scr[1, :, 0:128] = grad[:, 128:256]
        gain = jnp.broadcast_to(row_sum, (D, HD))
        scr[0, :, 128:256] = jnp.concatenate([grad[:, 256 : 256 + HD], gain], axis=1)
        scr[1, :, 128:256] = jnp.concatenate([grad[:, 256 + HD : 384], gain], axis=1)
        repack(places, rows, scr, (keep1, send1))
        repack(places2, rows, scr, (keep2, send2), 256 + fs)


def attend_back(qkv_ref, probs_ref, hg_ref, grad_ref, grad_all, at):
    low = low_lanes()
    units = [(i, c) for i in range(PER) for c in range(3)]

    def enter(i, c):
        do = both_heads(hg_ref[i, :, c * 128 : c * 128 + 128], low)
        return dot(qkv_ref[i, :, lanes(2, c)], do, NT), do

    ahead = enter(*units[0])
    for j, (i, c) in enumerate(units):
        dp, do = ahead
        if j + 1 < len(units):
            ahead = enter(*units[j + 1])
        low_probs = probs_ref[i, c]
        probs = low_probs.astype(F32)
        weighted = probs * dp
        ds = (weighted - probs * jnp.sum(weighted, axis=0, keepdims=True)).astype(BF16)
        q, k = qkv_ref[i, :, lanes(0, c)], qkv_ref[i, :, lanes(1, c)]
        dv = dot(low_probs, do)
        dk = dot(ds, both_heads(q, low))
        dq = own_heads(dot(k.T, ds)) * (HD**-0.5)
        for kind, value in enumerate((dq, dk, dv)):
            value = value.astype(BF16)
            grad_ref[i, :, lanes(kind, c)] = value
            if grad_all is not None:
                grad_all[pl.ds(pl.multiple_of(at + i * PAD, PAD), PAD), lanes(kind, c)] = value


def attend_back_kernel(qkv_ref, probs_ref, hg_ref, grad_ref):
    attend_back(qkv_ref, probs_ref, hg_ref, grad_ref, None, 0)


def attend_last_kernel(
    places, rows, blocks, qkv_ref, probs_ref, hg_ref, n1_ref, w_ref, *refs
):
    *earlier, grad_ref, keep, send, scr, grad_all = refs
    step = pl.program_id(0)
    early = sum(ref.shape[0] for ref in earlier) * PAD

    @pl.when(step == 0)
    def _():
        at = 0
        for ref in earlier:
            size = ref.shape[0] * PAD
            grad_all[at : at + size, :] = ref[...].reshape(size, 3 * D)
            at += size

    @pl.when(step < blocks)
    def _():
        attend_back(qkv_ref, probs_ref, hg_ref, grad_ref, grad_all, early + step * PER * PAD)

    @pl.when(step == blocks)
    def _():
        turned = n1_ref[...].reshape(-1, D).T
        row_sum = jnp.zeros((D, 1), F32)
        singles = [None] * 3
        for b in (8, 4, 0):
            some = range(b, min(b + 4, 9))
            span = slice(b * 128, some.stop * 128)
            grad = dot(turned, grad_all[:, span])
            row_sum += jnp.sum(grad * w_ref[:, span].astype(F32), axis=1, keepdims=True)
            for at in some:
                here = grad[:, (at - b) * 128 : (at - b) * 128 + 128]
                if at < 6:
                    scr[at // 3, :, at % 3 * 128 : at % 3 * 128 + 128] = here
                else:
                    singles[at - 6] = here
            if b == 4:
                for t in range(2):
                    own = [s[:, t * HD : t * HD + HD] for s in singles]
                    scr[t, :, 384:512] = jnp.concatenate(own[:2], axis=1)
                    scr[t, :, 512 : 512 + HD] = own[2]
        scr[:, :, 512 + HD : 640] = jnp.broadcast_to(row_sum[None], (2, D, HD))
        repack(places, rows, scr, (keep, send))


def store_rows(ref, value, step, steps):
    for s in range(steps):

        @pl.when(step == s)
        def _(s=s):
            for i in range(PER):
                at = (s * PER + i) * SEQ
                ref[at : at + SEQ, :] = value[i * PAD : i * PAD + SEQ]


def input_grad_kernel(cuts, *refs):
    *pieces, w_ref, x_ref, mg_ref, gain_ref, out_ref, w_turned, grad = refs
    step = pl.program_id(0)

    @pl.when(step == 0)
    def _():
        w_turned[:, :D] = w_ref[...].T
        w_turned[:, D:] = jnp.zeros((w_turned.shape[0], WIDE - D), BF16)

    at = 0
    for ref, count in zip(pieces, cuts, strict=True):

        @pl.when((step >= at) & (step < at + count))
        def _(ref=ref):
            grad[...] = tall(ref)

        at += count
    xhat, rstd = normalize(tall(x_ref).astype(F32))
    back = dot(grad[...], w_turned[...])[:, :D]
    dx = tall(mg_ref).astype(F32) + norm_back(back, xhat, rstd, gain_ref[0:1, :])
    store_rows(out_ref, dx, step, sum(cuts))


def finish_kernel(fs, mine_q, got_q, mine, got, gain1, gain2, ln1, qkv_grad, ln2, out_grad, fc1_grad, fc2_grad):
    total = mine_q[0].astype(F32) + got_q[0].astype(F32)
    for c in range(3):
        qkv_grad[c, :, 0:128] = total[:, c * 128 : c * 128 + 128]
        qkv_grad[c, :, 128:192] = total[:, 384 + c * HD : 448 + c * HD]
    ln1[...] = line(total[:, 576:577]) / gain1[...].astype(BF16).astype(F32)
    total = mine[0].astype(F32) + got[0].astype(F32)
    out_grad[...] = total[:, :192]
    fc1_grad[...] = total[:, 256 : 256 + fs]
    fc2_grad[...] = total[:, 256 + fs :]
    ln2[...] = line(total[:, 192:193]) / gain2[...].astype(BF16).astype(F32)


def whole(*shape):
    return pl.BlockSpec(shape, lambda *i: (0,) * len(shape))


def once(*shape):
    return pl.BlockSpec(shape, lambda *i: (0,) * len(shape), pipeline_mode=pl.Buffered(1))


def part(first, count, *shape):
    return pl.BlockSpec((PER,) + shape, lambda i: (first + jnp.minimum(i, count - 1),) + (0,) * len(shape))


def late(first, count, *shape):
    return pl.BlockSpec((PER,) + shape, lambda i: (jnp.clip(i - first, 0, count - 1),) + (0,) * len(shape))


def call(kernel, grid, ins, outs, scratch, args, mflops=0, kbytes=0, vmem=8):
    return pl.pallas_call(
        kernel,
        grid=(grid,) if grid else (),
        in_specs=ins,
        out_specs=[spec for spec, _ in outs],
        out_shape=[shape for _, shape in outs],
        scratch_shapes=scratch,
        compiler_params=pltpu.CompilerParams(vmem_limit_bytes=vmem * 1024 * 1024),
        cost_estimate=pl.CostEstimate(flops=mflops * 10**6, bytes_accessed=kbytes * 1000, transcendentals=0),
    )(*args)


def shape_of(*shape, dtype=BF16):
    return jax.ShapeDtypeStruct(shape, dtype)


def local(sizes, tokens, ln1_gain, qkv_weight, out_weight, ln2_gain, fc1_weight, fc2_weight, out_grad):
    return layer(sizes, tokens, ln1_gain, qkv_weight, out_weight, ln2_gain, fc1_weight, fc2_weight, out_grad)


def layer(sizes, tokens, ln1_gain, qkv_weight, out_weight, ln2_gain, fc1_weight, fc2_weight, out_grad):
    stages = stage_bits(sizes["wide"])
    stages2 = stages[:-3] + [stages[-2], stages[-3], stages[-1]]
    places, places2 = relative(stages), relative(stages2)
    n = len(places)
    rows = own_rows = qkv_weight.shape[0]
    images = tokens.shape[0] // SEQ
    blocks = images // PER
    fs = fc1_weight.shape[1]
    ff = 2 * fs
    rc = 256 + 2 * fs
    big = images * PAD
    gain1, gain2 = ln1_gain.reshape(1, rows), ln2_gain.reshape(1, rows)

    first, rest1, rest2 = call(
        pack_kernel,
        0,
        [whole(3, rows, 192), whole(1, rows), whole(1, rows), whole(rows, 192), whole(rows, fs), whole(rows, fs)],
        [(whole(1, rows, w), shape_of(1, rows, w)) for w in (QC, 256 + fs, fs)],
        [],
        tuple(pltpu.with_memory_space_constraint(v, pltpu.HBM) for v in (qkv_weight.transpose(1, 0, 2), gain1, gain2, out_weight.T, fc1_weight, fc2_weight.T)),
    )
    first_all = gather(first, stages, sizes)
    rest1_all = gather(rest1, stages2, sizes)
    rest2_all = gather(rest2, stages, sizes)
    if rows % 8 != 0:
        n, rows = 16, 48
        first_all, rest1_all, rest2_all = (
            jnp.split(in_order(order, jnp.concatenate(v, axis=0)), 4)
            for order, v in ((places, first_all), (places2, rest1_all), (places, rest2_all))
        )

    x, og = call(
        pad_kernel,
        0,
        [whole(images * SEQ, D)] * 2,
        [(whole(images, PAD, D), shape_of(images, PAD, D))] * 2,
        [],
        (tokens, out_grad),
        2000,
        10000,
        12,
    )

    def row(*shape):
        return part(0, blocks, *shape)

    qkv, probs, heads, n1, w_qkv, gain = call(
        functools.partial(attend_kernel, places, rows),
        blocks,
        [once(n // 4, rows, QC)] * 4 + [row(PAD, D)],
        [
            (row(PAD, 3 * D), shape_of(images, PAD, 3 * D)),
            (row(3, PAD, WIDE), shape_of(images, 3, PAD, WIDE)),
            (row(PAD, D), shape_of(images, PAD, D)),
            (row(PAD, D), shape_of(images, PAD, D)),
            (whole(D, 3 * D), shape_of(D, 3 * D)),
            (whole(8, D), shape_of(8, D, dtype=F32)),
        ],
        [pltpu.VMEM((2, D, QC), F32)],
        (*first_all, x),
        8000,
        20000,
        12,
    )
    wide1, wide2 = 256 + fs, fs
    y, mg, hg, keep1, send1, keep2, send2 = call(
        functools.partial(mlp_kernel, places, places2, rows, blocks, fs),
        blocks + 1,
        [once(n // 4, rows, wide1)] * 4
        + [once(n // 4, rows, wide2)] * 4
        + [row(PAD, D), row(PAD, D), row(PAD, D), whole(8, D)],
        [
            (once(images * SEQ, D), shape_of(images * SEQ, D)),
            (row(PAD, D), shape_of(images, PAD, D)),
            (row(PAD, D), shape_of(images, PAD, D)),
        ]
        + [(once(n // 2, rows, w), shape_of(n // 2, rows, w)) for w in (wide1, wide1, wide2, wide2)],
        [
            pltpu.VMEM((2, D, rc), F32),
            pltpu.VMEM((D, D), BF16),
            pltpu.VMEM((D, ff), BF16),
            pltpu.VMEM((D, ff), BF16),
            pltpu.VMEM((big, D), BF16),
            pltpu.VMEM((big, ff), BF16),
            pltpu.VMEM((big, ff), BF16),
            pltpu.VMEM((big, D), BF16),
            pltpu.VMEM((big, D), BF16),
            pltpu.VMEM((big, WIDE), BF16),
        ],
        (*rest1_all, *rest2_all, x, og, heads, gain),
        16000,
        30000,
        34,
    )
    if rows != own_rows:
        keep1, send1 = jnp.split(out_of_order(places, jnp.concatenate([keep1, send1], axis=0), own_rows), 2)
        keep2, send2 = jnp.split(out_of_order(places2, jnp.concatenate([keep2, send2], axis=0), own_rows), 2)
    back, back2 = stages[::-1], stages2[::-1]
    total1 = add_got(keep1, swap(send1, back[0], sizes))
    total2 = add_got(keep2, swap(send2, back[0], sizes))
    for s in (1, 2):
        total1 = reduce_stage(total1, back[s], sizes)
        total2 = reduce_stage(total2, back2[s], sizes)
    total = jnp.concatenate([total1, total2], axis=2)
    for stage in back[3:-1]:
        total = reduce_stage(total, stage, sizes)
    got = swap(total[1:], back[-1], sizes)

    cuts = (blocks // 2, blocks - blocks // 2)
    pieces = []
    at = 0
    for count in cuts[:-1]:
        pieces += call(
            attend_back_kernel,
            count,
            [part(at, count, *s) for s in ((PAD, 3 * D), (3, PAD, WIDE), (PAD, D))],
            [(part(0, count, PAD, 3 * D), shape_of(count * PER, PAD, 3 * D))],
            [],
            (qkv, probs, hg),
            1800 * count,
            4000 * count,
            8,
        )
        at += count
    left = cuts[-1]
    last, keep_q, send_q = call(
        functools.partial(attend_last_kernel, places, rows, left),
        left + 1,
        [part(at, left, *s) for s in ((PAD, 3 * D), (3, PAD, WIDE), (PAD, D))]
        + [once(images, PAD, D), once(D, 3 * D)]
        + [once(count * PER, PAD, 3 * D) for count in cuts[:-1]],
        [(part(0, left, PAD, 3 * D), shape_of(left * PER, PAD, 3 * D))]
        + [(whole(n // 2, rows, QC), shape_of(n // 2, rows, QC))] * 2,
        [pltpu.VMEM((2, D, QC), F32), pltpu.VMEM((big, 3 * D), BF16)],
        (qkv, probs, hg, n1, w_qkv, *pieces),
        3500,
        8000,
        14,
    )
    pieces.append(last)
    starts = [sum(cuts[:c]) for c in range(len(cuts))]
    (dx,) = call(
        functools.partial(input_grad_kernel, cuts),
        blocks,
        [late(at, count, PAD, 3 * D) for at, count in zip(starts, cuts, strict=True)]
        + [whole(D, 3 * D), row(PAD, D), row(PAD, D), whole(8, D)],
        [(once(images * SEQ, D), shape_of(images * SEQ, D, dtype=F32))],
        [pltpu.VMEM((3 * D, WIDE), BF16), pltpu.VMEM((PER * PAD, 3 * D), BF16)],
        (*pieces, w_qkv, x, mg, gain),
        2000,
        10000,
        10,
    )
    if rows != own_rows:
        keep_q, send_q = jnp.split(out_of_order(places, jnp.concatenate([keep_q, send_q], axis=0), own_rows), 2)
    total_q = add_got(keep_q, swap(send_q, back[0], sizes))
    for stage in back[1:-1]:
        total_q = reduce_stage(total_q, stage, sizes)
    got_q = swap(total_q[1:], back[-1], sizes)
    ln1_grad, qkv_grad, ln2_grad, out_wgrad, fc1_grad, fc2_grad = call(
        functools.partial(finish_kernel, fs),
        0,
        [whole(2, own_rows, QC), whole(1, own_rows, QC), whole(2, own_rows, rc), whole(1, own_rows, rc)]
        + [whole(1, own_rows)] * 2,
        [
            (whole(*shape), shape_of(*shape, dtype=F32))
            for shape in (
                (1, own_rows),
                (3, own_rows, 192),
                (1, own_rows),
                (own_rows, 192),
                (own_rows, fs),
                (own_rows, fs),
            )
        ],
        [],
        (total_q, got_q, total, got, gain1, gain2),
    )
    return (
        y,
        dx,
        ln1_grad.reshape(own_rows),
        qkv_grad.transpose(1, 0, 2),
        out_wgrad.T,
        ln2_grad.reshape(own_rows),
        fc1_grad,
        fc2_grad.T,
    )


def solution(mesh):
    rows = P(("wide", "tensor"), None)
    weights = (
        P("wide"),
        P("wide", None, "tensor"),
        P("tensor", "wide"),
        P("wide"),
        P("wide", "tensor"),
        P("tensor", "wide"),
    )
    return jax.shard_map(
        functools.partial(local, dict(mesh.shape)),
        mesh=mesh,
        in_specs=(rows, *weights, rows),
        out_specs=(rows, rows, *weights),
        check_vma=False,
    )
```
